32 devices in a mesh: along: 8 (over y, x, core), across: 4 (over z).
Axes of the slice: x: 2, y: 2, z: 4, core: 2. Of those that a mesh axis runs over, the one named last changes fastest.
Arguments:
- fields: float32 [40, 3, 32, 4096], P(None, None, 'across', 'along'), may hold values from -6 to 6
- first_feet: int32 [32, 4096], P('across', 'along'), may hold values from 0 to 131071, as said below
- first_fraction: float32 [40, 32, 4096], P(None, 'across', 'along'), may hold values from 0 to 1
- second_feet: int32 [32, 4096], P('across', 'along'), may hold values from 0 to 131071, as said below
- second_fraction: float32 [40, 32, 4096], P(None, 'across', 'along'), may hold values from 0 to 1
- lateral_mix: float32 [32, 4096], P('across', 'along'), may hold values from 0.02 to 0.2
- vertical_mix: float32 [2, 39, 32, 4096], P(None, None, 'across', 'along'), may hold values from 0.05 to 5
- bottom_drag: float32 [32, 4096], P('across', 'along'), may hold values from 0.05 to 2
- surface_stress: float32 [2, 32, 4096], P(None, 'across', 'along'), may hold values from -3 to 3
Outputs:
- advanced: float32 [40, 3, 32, 4096], P(None, None, 'across', 'along')
The draws below stay inside these ranges and needn't reach their ends.
Inputs may be any that keep to these rules, and one draw needn't show every extreme that they name: `first_feet`: A cell in the block of 8 x 512 cells with along block index a has its foot point (row p // 4096, column p % 4096) in a block whose along index lies from w to w + 1 - 1, w = max(a - 1 + 1, 0), at any cross block index. At most 1152 cells of one block have foot points in one block, and some pair of blocks reaches 1152. `second_feet`: as for first_feet.
All inputs are finite; a program needn't handle non-finite values.
Results may differ from the reference program's by a relative error of at most 0.00002.
Values sent between devices are 32-bit elements; how exact they have to be, the bound alone decides.
A program may use at most 64 MiB of HBM per device.

```python
import math
import jax
import jax.numpy as jnp

LAYERS = 40
CROSS_DEV = 8
ALONG_DEV = 512
REACH = 1
CAPACITY = 1152
CELLS_ACROSS = 32
CELLS_ALONG = 4096


def make_feet(key):
    along_count = CELLS_ALONG // ALONG_DEV
    across_count = CELLS_ACROSS // CROSS_DEV
    cells_dev = CROSS_DEV * ALONG_DEV
    partners = across_count * REACH
    slot_total = partners * CAPACITY
    subkeys = jax.random.split(key, 6)
    hot_along = jax.random.randint(subkeys[0], (), 0, along_count)
    hot_across = jax.random.randint(subkeys[1], (), 0, across_count)
    window = jnp.maximum(jnp.arange(along_count) - REACH + 1, 0)
    has_hot = (hot_along >= window) & (hot_along < window + REACH)
    hot_slot = (hot_along - window) * across_count + hot_across
    random_slot = jax.random.randint(subkeys[2], (across_count, along_count), 0, partners)
    full_slot = jnp.where(has_hot[None, :], hot_slot[None, :], random_slot)
    labels = jnp.arange(slot_total) // CAPACITY
    scores = jax.random.randint(subkeys[3], (across_count, along_count, slot_total), 0, 4096) * slot_total + jnp.arange(slot_total)
    scores = jnp.where(labels == full_slot[..., None], jnp.arange(slot_total) - slot_total, scores)
    chosen = labels[jnp.argsort(scores, axis=-1)[..., :cells_dev]]
    shuffle = jax.random.randint(subkeys[4], (across_count, along_count, cells_dev), 0, 4096) * cells_dev + jnp.arange(cells_dev)
    chosen = jnp.take_along_axis(chosen, jnp.argsort(shuffle, axis=-1), axis=-1)
    owner_along = window[None, :, None] + chosen // across_count
    owner_across = chosen % across_count
    local_cell = jax.random.randint(subkeys[5], (across_count, along_count, cells_dev), 0, cells_dev)
    global_id = (owner_across * CROSS_DEV + local_cell // ALONG_DEV) * CELLS_ALONG + owner_along * ALONG_DEV + local_cell % ALONG_DEV
    arranged = global_id.reshape(across_count, along_count, CROSS_DEV, ALONG_DEV).transpose(0, 2, 1, 3)
    return arranged.reshape(CELLS_ACROSS, CELLS_ALONG).astype(jnp.int32)


def draw_first_feet(key, part):
    return make_feet(jax.random.fold_in(key, 11))


def draw_second_feet(key, part):
    return make_feet(jax.random.fold_in(key, 23))


def block_levels(stream_key, shape, cuts, smallest, high):
    gain, own = 1.0, jax.random.fold_in(stream_key, 6)
    for dim, blocks in cuts:
        steps = jnp.exp(jax.random.uniform(jax.random.fold_in(own, dim), (blocks,), jnp.float32, smallest / len(cuts), high / len(cuts)))
        gain = gain * jnp.repeat(steps, shape[dim] // blocks).reshape([-1 if axis == dim else 1 for axis in range(len(shape))])
    return gain


def scatter_about(stream_key, dims, deviation, bound, cuts=(), kind=jnp.bfloat16):
    gain = block_levels(stream_key, dims, cuts, -0.22, 0.18) if cuts else 1.0
    values = jax.random.normal(stream_key, dims, jnp.float32) * deviation * gain
    return jnp.minimum(jnp.maximum(values, -bound), bound).astype(kind)


def setup_inputs(seed: int = 0) -> dict:
    streams_of = jax.random.split(jax.random.key(seed), 10)
    return {
        "fields": scatter_about(streams_of[0], (LAYERS, 3, CELLS_ACROSS, CELLS_ALONG), 1.0, 6.0, ((2, 4), (3, 8)), jnp.float32),
        "first_feet": draw_first_feet(jax.random.fold_in(streams_of[9], 71), 0),
        "first_fraction": jnp.clip(1.0 * jax.random.uniform(streams_of[2], (LAYERS, CELLS_ACROSS, CELLS_ALONG), jnp.float32) ** block_levels(streams_of[2], (LAYERS, CELLS_ACROSS, CELLS_ALONG), ((1, 4), (2, 8)), -0.2, 0.2), 0.0, 1.0),
        "second_feet": draw_second_feet(jax.random.fold_in(streams_of[9], 71), 0),
        "second_fraction": jnp.clip(1.0 * jax.random.uniform(streams_of[4], (LAYERS, CELLS_ACROSS, CELLS_ALONG), jnp.float32) ** block_levels(streams_of[4], (LAYERS, CELLS_ACROSS, CELLS_ALONG), ((1, 4), (2, 8)), -0.2, 0.2), 0.0, 1.0),
        "lateral_mix": jnp.clip(jnp.exp(math.log(0.2) - 2.3025851 * jax.random.uniform(streams_of[5], (CELLS_ACROSS, CELLS_ALONG), jnp.float32) ** block_levels(streams_of[5], (CELLS_ACROSS, CELLS_ALONG), ((0, 4), (1, 8)), -0.2, 0.2)), 0.02, 0.2),
        "vertical_mix": jnp.clip(jnp.exp(math.log(5.0) - 4.6051702 * jax.random.uniform(streams_of[6], (2, LAYERS - 1, CELLS_ACROSS, CELLS_ALONG), jnp.float32) ** block_levels(streams_of[6], (2, LAYERS - 1, CELLS_ACROSS, CELLS_ALONG), ((2, 4), (3, 8)), -0.2, 0.2)), 0.05, 5.0),
        "bottom_drag": jnp.clip(jnp.exp(math.log(2.0) - 3.6888794 * jax.random.uniform(streams_of[7], (CELLS_ACROSS, CELLS_ALONG), jnp.float32) ** block_levels(streams_of[7], (CELLS_ACROSS, CELLS_ALONG), ((0, 4), (1, 8)), -0.2, 0.2)), 0.05, 2.0),
        "surface_stress": scatter_about(streams_of[8], (2, CELLS_ACROSS, CELLS_ALONG), 0.5, 3.0, ((1, 4), (2, 8)), jnp.float32),
    }


def interpolate(columns, fraction):
    upper = jnp.concatenate([columns[1:], columns[-1:]], axis=0)
    weight = fraction[:, None]
    return (1.0 - weight) * columns + weight * upper


def neighbour_sum(padded):
    total = padded[:, :, :-2, 1:-1] + padded[:, :, 2:, 1:-1]
    return total + padded[:, :, 1:-1, :-2] + padded[:, :, 1:-1, 2:]


def solve_columns(forcing, vertical_mix, bottom_drag, surface_stress):
    layers = forcing.shape[0]
    coupling = jnp.stack([vertical_mix[0], vertical_mix[0], vertical_mix[1]], axis=1)
    nothing = jnp.zeros_like(coupling[:1])
    below = jnp.concatenate([nothing, coupling], axis=0)
    above = jnp.concatenate([coupling, nothing], axis=0)
    friction = jnp.stack([bottom_drag, bottom_drag, jnp.zeros_like(bottom_drag)], axis=0)
    diagonal = (1.0 + below + above).at[0].add(friction)
    source = forcing.at[layers - 1, 0:2].add(surface_stress)
    factor = above[0] / diagonal[0]
    partial_value = source[0] / diagonal[0]
    factors = [factor]
    partials = [partial_value]
    for level_index in range(1, layers):
        denominator = diagonal[level_index] - below[level_index] * factor
        factor = above[level_index] / denominator
        partial_value = (source[level_index] + below[level_index] * partial_value) / denominator
        factors.append(factor)
        partials.append(partial_value)
    solution = partials[layers - 1]
    results = [solution]
    for level_index in range(layers - 2, -1, -1):
        solution = partials[level_index] + factors[level_index] * solution
        results.append(solution)
    return jnp.stack(results[::-1], axis=0)


def reference(fields, first_feet, first_fraction, second_feet, second_fraction, lateral_mix, vertical_mix, bottom_drag, surface_stress):
    layers, components, row_total, column_total = fields.shape

    def advect(current, feet, fraction):
        flattened = current.reshape(layers * components, row_total * column_total)
        gathered = jnp.take(flattened, feet.reshape(-1).astype(jnp.int32), axis=1)
        return interpolate(gathered.reshape(layers, components, row_total, column_total), fraction)

    middle = advect(fields, first_feet, first_fraction)
    moved = advect(middle, second_feet, second_fraction)
    padded = jnp.pad(moved, ((0, 0), (0, 0), (1, 1), (1, 1)))
    beside_all = neighbour_sum(padded)
    row_index = jnp.arange(row_total, dtype=jnp.int32)
    column_index = jnp.arange(column_total, dtype=jnp.int32)
    row_count = (row_index > 0).astype(jnp.float32) + (row_index < row_total - 1).astype(jnp.float32)
    column_count = (column_index > 0).astype(jnp.float32) + (column_index < column_total - 1).astype(jnp.float32)
    present = row_count[:, None] + column_count[None, :]
    mixed = moved + lateral_mix * (beside_all - present * moved)
    return solve_columns(mixed, vertical_mix, bottom_drag, surface_stress)
```

```python
import functools

import jax
import jax.numpy as jnp
from jax import lax
from jax.experimental import pallas as pl
from jax.experimental.pallas import tpu as pltpu
from jax.sharding import PartitionSpec as P


def shifted(block, axis, distance):
    devices = range(lax.axis_size(axis))
    route = [(i - distance, i) for i in devices if i - distance in devices]
    return lax.ppermute(block, axis, route)


def padded_2(value, sides, width):
    for axis, dim in sides:
        count, length = (lax.axis_size(axis), value.shape[dim])
        up = [(i, (i + 1) % count) for i in range(count - 1)]
        down = [(j, i) for i, j in up]
        last = lax.slice_in_dim(value, length - width, length, axis=dim)
        first = lax.slice_in_dim(value, 0, width, axis=dim)
        before = lax.ppermute(last, axis, up)
        after = lax.ppermute(first, axis, down)
        value = jnp.concatenate([before, value, after], axis=dim)
    return value


def neighbour_sum(padded):
    total = padded[:, :, :-2, 1:-1] + padded[:, :, 2:, 1:-1]
    return total + padded[:, :, 1:-1, :-2] + padded[:, :, 1:-1, 2:]


def solve_columns(forcing, vertical_mix, bottom_drag, surface_stress):
    layers = forcing.shape[0]
    coupling = jnp.stack([vertical_mix[0], vertical_mix[0], vertical_mix[1]], axis=1)
    nothing = jnp.zeros_like(coupling[:1])
    below = jnp.concatenate([nothing, coupling], axis=0)
    above = jnp.concatenate([coupling, nothing], axis=0)
    friction = jnp.stack([bottom_drag, bottom_drag, jnp.zeros_like(bottom_drag)], axis=0)
    diagonal = (1.0 + below + above).at[0].add(friction)
    source = forcing.at[layers - 1, 0:2].add(surface_stress)
    factor = above[0] / diagonal[0]
    partial_value = source[0] / diagonal[0]
    factors = [factor]
    partials = [partial_value]
    for level_index in range(1, layers):
        denominator = diagonal[level_index] - below[level_index] * factor
        factor = above[level_index] / denominator
        partial_value = (source[level_index] + below[level_index] * partial_value) / denominator
        factors.append(factor)
        partials.append(partial_value)
    solution = partials[layers - 1]
    results = [solution]
    for level_index in range(layers - 2, -1, -1):
        solution = partials[level_index] + factors[level_index] * solution
        results.append(solution)
    return jnp.stack(results[::-1], axis=0)


def owners(feet, cross_dev, along_dev, along_total):
    flat_feet = feet.reshape(-1)
    global_row = flat_feet // along_total
    global_column = flat_feet % along_total
    local_cell = global_row % cross_dev * along_dev + global_column % along_dev
    return (global_column // along_dev, global_row // cross_dev, local_cell)


def prefix_count(member):
    partners, cells = member.shape
    lanes = 128
    blocks = member.reshape(partners, cells // lanes, lanes)
    before = jnp.triu(jnp.ones((lanes, lanes), jnp.bfloat16), 1)
    inside = lax.dot_general(
        blocks.astype(jnp.bfloat16), before, (((2,), (0,)), ((), ())),
        preferred_element_type=jnp.float32,
    ).astype(jnp.int32)
    totals = blocks.sum(axis=2)
    ahead = jnp.cumsum(totals, axis=1) - totals
    return (inside + ahead[:, :, None]).reshape(partners, cells), totals.sum(axis=1)


def plan(feet, cross_dev, along_dev):
    along_count = lax.axis_size("along")
    across_count = lax.axis_size("across")
    cells = cross_dev * along_dev
    reach = along_count // 8
    capacity = 9 * cells // (8 * across_count * reach)
    span = 2 * reach - 1
    partners = across_count * span
    owner_along, owner_across, local_cell = owners(
        feet, cross_dev, along_dev, along_dev * along_count
    )
    offset = owner_along - lax.axis_index("along")
    partner = owner_across * span + offset + reach - 1
    member = (partner[None, :] == jnp.arange(partners, dtype=jnp.int32)[:, None]).astype(jnp.int32)
    rank, counts = prefix_count(member)
    target = jnp.sum(
        member * (rank + capacity * jnp.arange(partners, dtype=jnp.int32)[:, None]), axis=0
    )
    key = (partner * cells + jnp.arange(cells, dtype=jnp.int32)) * cells + local_cell
    ordered = jnp.pad(lax.sort(key) % cells, (0, capacity))
    starts = jnp.cumsum(counts) - counts
    requests = jnp.stack(
        [lax.dynamic_slice(ordered, (starts[p],), (capacity,)) for p in range(partners)]
    )
    return requests.reshape(across_count, span, capacity), target


def hop_groups(reach, power):
    upward = [offset + reach - 1 for offset in range(1 - reach, 0) if -offset >> power & 1]
    downward = [offset + reach - 1 for offset in range(1, reach) if offset >> power & 1]
    return (upward, downward)


UNROLL = 32


def gather_kernel(index_ref, table_ref, out_ref):
    def step(i, carry):
        base = pl.multiple_of(i * UNROLL, UNROLL)
        for u in range(UNROLL):
            out_ref[pl.ds(base + u, 1), :] = table_ref[pl.ds(index_ref[base + u], 1), :]
        return carry

    lax.fori_loop(0, out_ref.shape[0] // UNROLL, step, 0)


def gather_rows(table, index):
    count, width = index.shape[0], table.shape[1]
    return pl.pallas_call(
        gather_kernel,
        out_shape=jax.ShapeDtypeStruct((count, width), table.dtype),
        in_specs=[
            pl.BlockSpec(memory_space=pltpu.SMEM),
            pl.BlockSpec(memory_space=pltpu.VMEM),
        ],
        out_specs=pl.BlockSpec(memory_space=pltpu.VMEM),
        name="gather_rows",
    )(index, table)


def blend_kernel(layers, index_ref, table_ref, fraction_ref, out_ref):
    width = out_ref.shape[1]
    lane = lax.broadcasted_iota(jnp.int32, (UNROLL, width), 1)
    top = lane % layers == layers - 1

    def step(i, carry):
        base = pl.multiple_of(i * UNROLL, UNROLL)
        for u in range(UNROLL):
            out_ref[pl.ds(base + u, 1), :] = table_ref[pl.ds(index_ref[base + u], 1), :]
        rows = out_ref[pl.ds(base, UNROLL), :]
        upper = jnp.where(top, rows, pltpu.roll(rows, width - 1, 1))
        weight = fraction_ref[pl.ds(base, UNROLL), :]
        out_ref[pl.ds(base, UNROLL), :] = (1.0 - weight) * rows + weight * upper
        return carry

    lax.fori_loop(0, out_ref.shape[0] // UNROLL, step, 0)


def blend_rows(table, index, fraction, layers):
    return pl.pallas_call(
        functools.partial(blend_kernel, layers),
        out_shape=jax.ShapeDtypeStruct(fraction.shape, table.dtype),
        in_specs=[
            pl.BlockSpec(memory_space=pltpu.SMEM),
            pl.BlockSpec(memory_space=pltpu.VMEM),
            pl.BlockSpec(memory_space=pltpu.VMEM),
        ],
        out_specs=pl.BlockSpec(memory_space=pltpu.VMEM),
        name="blend_rows",
    )(index, table, fraction)


def to_holders(requests):
    reach = (requests.shape[1] + 1) // 2
    moved = lax.all_to_all(requests, "across", split_axis=0, concat_axis=0, tiled=True)
    for power in range((reach - 1).bit_length()):
        upward, downward = hop_groups(reach, power)
        moved = moved.at[:, upward].set(shifted(moved[:, upward], "along", -(1 << power)))
        moved = moved.at[:, downward].set(shifted(moved[:, downward], "along", 1 << power))
    return moved


def to_askers(picked):
    reach = (picked.shape[1] + 1) // 2
    for power in range((reach - 1).bit_length()):
        upward, downward = hop_groups(reach, power)
        picked = picked.at[:, upward].set(shifted(picked[:, upward], "along", 1 << power))
        picked = picked.at[:, downward].set(shifted(picked[:, downward], "along", -(1 << power)))
    return lax.all_to_all(picked, "across", split_axis=0, concat_axis=0, tiled=True)


def body(
    fields,
    first_feet,
    first_fraction,
    second_feet,
    second_fraction,
    lateral_mix,
    vertical_mix,
    bottom_drag,
    surface_stress,
):
    layers, components, cross_dev, along_dev = fields.shape
    cells = cross_dev * along_dev
    row_count = layers * components
    width = (row_count + 127) // 128 * 128

    first_requests, first_target = plan(first_feet, cross_dev, along_dev)
    second_requests, second_target = plan(second_feet, cross_dev, along_dev)
    capacity = first_requests.shape[2]
    asked = to_holders(jnp.concatenate([first_requests, second_requests], axis=2))

    def advect(table, asked, target, fraction):
        weight = jnp.pad(
            jnp.tile(fraction.reshape(layers, cells), (components, 1)),
            ((0, width - row_count), (0, 0)),
        ).T
        picked = gather_rows(table, asked.reshape(-1))
        returned = to_askers(picked.reshape(asked.shape + (width,)))
        return blend_rows(returned.reshape(-1, width), target, weight, layers)

    table = fields.transpose(1, 0, 2, 3).reshape(row_count, cells)
    table = jnp.pad(table, ((0, width - row_count), (0, 0))).T
    middle = advect(table, asked[:, :, :capacity], first_target, first_fraction)
    moved = advect(middle, asked[:, :, capacity:], second_target, second_fraction)
    moved = moved.T[:row_count].reshape(components, layers, cross_dev, along_dev)
    moved = moved.transpose(1, 0, 2, 3)
    padded = padded_2(moved, (("across", 2), ("along", 3)), 1)
    beside_all = neighbour_sum(padded)
    row_total = cross_dev * lax.axis_size("across")
    column_total = along_dev * lax.axis_size("along")
    row_index = lax.axis_index("across") * cross_dev + jnp.arange(cross_dev, dtype=jnp.int32)
    column_index = lax.axis_index("along") * along_dev + jnp.arange(along_dev, dtype=jnp.int32)
    row_present = (row_index > 0).astype(jnp.float32) + (row_index < row_total - 1).astype(
        jnp.float32
    )
    column_present = (column_index > 0).astype(jnp.float32) + (
        column_index < column_total - 1
    ).astype(jnp.float32)
    present = row_present[:, None] + column_present[None, :]
    mixed = moved + lateral_mix * (beside_all - present * moved)
    return solve_columns(mixed, vertical_mix, bottom_drag, surface_stress)


def solution(mesh):
    in_specs = (
        P(None, None, "across", "along"),
        P("across", "along"),
        P(None, "across", "along"),
        P("across", "along"),
        P(None, "across", "along"),
        P("across", "along"),
        P(None, None, "across", "along"),
        P("across", "along"),
        P(None, "across", "along"),
    )
    out_specs = P(None, None, "across", "along")
    return jax.shard_map(body, mesh=mesh, in_specs=in_specs, out_specs=out_specs, check_vma=False)
```

```python
import functools

import jax
import jax.numpy as jnp
from jax import lax
from jax.experimental import pallas as pl
from jax.experimental.pallas import tpu as pltpu
from jax.sharding import PartitionSpec as P


def shifted(block, axis, distance):
    devices = range(lax.axis_size(axis))
    route = [(i - distance, i) for i in devices if i - distance in devices]
    return lax.ppermute(block, axis, route)


def padded_2(value, sides, width):
    for axis, dim in sides:
        count, length = (lax.axis_size(axis), value.shape[dim])
        up = [(i, (i + 1) % count) for i in range(count - 1)]
        down = [(j, i) for i, j in up]
        last = lax.slice_in_dim(value, length - width, length, axis=dim)
        first = lax.slice_in_dim(value, 0, width, axis=dim)
        before = lax.ppermute(last, axis, up)
        after = lax.ppermute(first, axis, down)
        value = jnp.concatenate([before, value, after], axis=dim)
    return value


def neighbour_sum(padded):
    total = padded[:, :, :-2, 1:-1] + padded[:, :, 2:, 1:-1]
    return total + padded[:, :, 1:-1, :-2] + padded[:, :, 1:-1, 2:]


def solve_columns(forcing, vertical_mix, bottom_drag, surface_stress):
    layers = forcing.shape[0]
    coupling = jnp.stack([vertical_mix[0], vertical_mix[0], vertical_mix[1]], axis=1)
    nothing = jnp.zeros_like(coupling[:1])
    below = jnp.concatenate([nothing, coupling], axis=0)
    above = jnp.concatenate([coupling, nothing], axis=0)
    friction = jnp.stack([bottom_drag, bottom_drag, jnp.zeros_like(bottom_drag)], axis=0)
    diagonal = (1.0 + below + above).at[0].add(friction)
    source = forcing.at[layers - 1, 0:2].add(surface_stress)
    factor = above[0] / diagonal[0]
    partial_value = source[0] / diagonal[0]
    factors = [factor]
    partials = [partial_value]
    for level_index in range(1, layers):
        denominator = diagonal[level_index] - below[level_index] * factor
        factor = above[level_index] / denominator
        partial_value = (source[level_index] + below[level_index] * partial_value) / denominator
        factors.append(factor)
        partials.append(partial_value)
    solution = partials[layers - 1]
    results = [solution]
    for level_index in range(layers - 2, -1, -1):
        solution = partials[level_index] + factors[level_index] * solution
        results.append(solution)
    return jnp.stack(results[::-1], axis=0)


def owners(feet, cross_dev, along_dev, along_total):
    flat_feet = feet
    global_row = flat_feet // along_total
    global_column = flat_feet % along_total
    local_cell = global_row % cross_dev * along_dev + global_column % along_dev
    return (global_column // along_dev, global_row // cross_dev, local_cell)


def prefix_count(member):
    partners, cells = member.shape
    lanes = 128
    blocks = member.reshape(partners, cells // lanes, lanes)
    before = jnp.triu(jnp.ones((lanes, lanes), jnp.bfloat16), 1)
    inside = lax.dot_general(
        blocks.astype(jnp.bfloat16), before, (((2,), (0,)), ((), ())),
        preferred_element_type=jnp.float32,
    ).astype(jnp.int32)
    totals = blocks.sum(axis=2)
    ahead = jnp.cumsum(totals, axis=1) - totals
    return (inside + ahead[:, :, None]).reshape(partners, cells), totals.sum(axis=1)


def plan(feet, cross_dev, along_dev):
    along_count = lax.axis_size("along")
    across_count = lax.axis_size("across")
    cells = cross_dev * along_dev
    reach = along_count // 8
    capacity = 9 * cells // (8 * across_count * reach)
    span = 2 * reach - 1
    partners = across_count * span
    substeps = feet.shape[0]
    owner_along, owner_across, local_cell = owners(
        feet.reshape(substeps, cells), cross_dev, along_dev, along_dev * along_count
    )
    offset = owner_along - lax.axis_index("along")
    partner = owner_across * span + offset + reach - 1
    key = (partner * cells + jnp.arange(cells, dtype=jnp.int32)) * cells + local_cell
    ordered = jnp.pad(lax.sort(key, dimension=1) % cells, ((0, 0), (0, capacity)))
    labels = jnp.arange(partners, dtype=jnp.int32)[:, None]
    member = (partner[:, None, :] == labels).astype(jnp.int32)
    rank, counts = prefix_count(member.reshape(substeps * partners, cells))
    rank = rank.reshape(substeps, partners, cells)
    target = jnp.sum(member * (rank + capacity * labels), axis=1)
    counts = counts.reshape(substeps, partners)
    starts = jnp.cumsum(counts, axis=1) - counts
    requests = [
        lax.dynamic_slice(ordered[s], (starts[s, p],), (capacity,))
        for p in range(partners)
        for s in range(substeps)
    ]
    return jnp.stack(requests).reshape(across_count, span, substeps, capacity), target


def hop_groups(reach, power):
    upward = [offset + reach - 1 for offset in range(1 - reach, 0) if -offset >> power & 1]
    downward = [offset + reach - 1 for offset in range(1, reach) if offset >> power & 1]
    return (upward, downward)


UNROLL = 32


def gather_kernel(index_ref, table_ref, out_ref):
    def step(i, carry):
        base = pl.multiple_of(i * UNROLL, UNROLL)
        for u in range(UNROLL):
            out_ref[pl.ds(base + u, 1), :] = table_ref[pl.ds(index_ref[base + u], 1), :]
        return carry

    lax.fori_loop(0, out_ref.shape[0] // UNROLL, step, 0)


def gather_rows(table, index):
    count, width = index.shape[0], table.shape[1]
    return pl.pallas_call(
        gather_kernel,
        out_shape=jax.ShapeDtypeStruct((count, width), table.dtype),
        in_specs=[
            pl.BlockSpec(memory_space=pltpu.SMEM),
            pl.BlockSpec(memory_space=pltpu.VMEM),
        ],
        out_specs=pl.BlockSpec(memory_space=pltpu.VMEM),
        name="gather_rows",
    )(index, table)


def blend_kernel(layers, index_ref, table_ref, fraction_ref, out_ref):
    width = out_ref.shape[1]
    lane = lax.broadcasted_iota(jnp.int32, (UNROLL, width), 1)
    top = lane % layers == layers - 1

    def step(i, carry):
        base = pl.multiple_of(i * UNROLL, UNROLL)
        for u in range(UNROLL):
            out_ref[pl.ds(base + u, 1), :] = table_ref[pl.ds(index_ref[base + u], 1), :]
        rows = out_ref[pl.ds(base, UNROLL), :]
        upper = jnp.where(top, rows, pltpu.roll(rows, width - 1, 1))
        weight = fraction_ref[pl.ds(base, UNROLL), :]
        out_ref[pl.ds(base, UNROLL), :] = (1.0 - weight) * rows + weight * upper
        return carry

    lax.fori_loop(0, out_ref.shape[0] // UNROLL, step, 0)


def blend_rows(table, index, fraction, layers):
    return pl.pallas_call(
        functools.partial(blend_kernel, layers),
        out_shape=jax.ShapeDtypeStruct(fraction.shape, table.dtype),
        in_specs=[
            pl.BlockSpec(memory_space=pltpu.SMEM),
            pl.BlockSpec(memory_space=pltpu.VMEM),
            pl.BlockSpec(memory_space=pltpu.VMEM),
        ],
        out_specs=pl.BlockSpec(memory_space=pltpu.VMEM),
        name="blend_rows",
    )(index, table, fraction)


def to_holders(requests):
    reach = (requests.shape[1] + 1) // 2
    moved = lax.all_to_all(requests, "across", split_axis=0, concat_axis=0, tiled=True)
    for power in range((reach - 1).bit_length()):
        upward, downward = hop_groups(reach, power)
        moved = moved.at[:, upward].set(shifted(moved[:, upward], "along", -(1 << power)))
        moved = moved.at[:, downward].set(shifted(moved[:, downward], "along", 1 << power))
    return moved


def to_askers(picked):
    reach = (picked.shape[1] + 1) // 2
    for power in range((reach - 1).bit_length()):
        upward, downward = hop_groups(reach, power)
        picked = picked.at[:, upward].set(shifted(picked[:, upward], "along", 1 << power))
        picked = picked.at[:, downward].set(shifted(picked[:, downward], "along", -(1 << power)))
    return lax.all_to_all(picked, "across", split_axis=0, concat_axis=0, tiled=True)


LANES = 128
PIECES = 3
MESH = pl.DeviceIdType.MESH


def blend(rows, weight, top):
    upper = jnp.where(top, rows, pltpu.roll(rows, rows.shape[1] - 1, 1))
    return (1.0 - weight) * rows + weight * upper


def exchange_kernel(
    layers,
    components,
    cross_dev,
    capacity,
    target_ref,
    requests_ref,
    fields_hbm,
    first_hbm,
    second_hbm,
    out_hbm,
    fields_ref,
    first_ref,
    second_ref,
    out_ref,
    asked_vmem,
    asked,
    table,
    first_rows,
    second_rows,
    sent_1,
    sent_2,
    back_1,
    back_2,
    stage,
    stage_weight,
    final,
    ask_send,
    ask_recv,
    ask_local,
    send_sem,
    recv_sem,
    load_sem,
):
    tiles = fields_ref.shape[0]
    along_dev = tiles * LANES
    cells = cross_dev * along_dev
    width = table.shape[1]
    blocks = capacity // LANES
    piece = capacity // PIECES
    along = lax.axis_index("along")
    me = lax.axis_index("across")
    peers = [lax.rem(me + 2, 4), 3 - me, me + 1 - 2 * lax.rem(me, 2)]
    pad = jnp.zeros((width - layers * components, LANES), jnp.float32)
    top = lax.broadcasted_iota(jnp.int32, (LANES, width), 1) % layers == layers - 1

    loads = [
        [
            pltpu.make_async_copy(
                source.at[:, pl.ds(t * LANES, LANES)], place.at[t], load_sem.at[s, t]
            )
            for t in range(tiles)
        ]
        for s, (source, place) in enumerate(
            [(fields_hbm, fields_ref), (first_hbm, first_ref), (second_hbm, second_ref)]
        )
    ]
    for group in loads:
        for copy in group:
            copy.start()

    barrier = pltpu.get_barrier_semaphore()
    for peer in peers:
        pl.semaphore_signal(barrier, inc=1, device_id=(along, peer), device_id_type=MESH)
    pl.semaphore_wait(barrier, 3)

    asks = []
    for j, peer in enumerate(peers):
        copy = pltpu.make_async_remote_copy(
            src_ref=requests_ref.at[peer],
            dst_ref=asked_vmem.at[me],
            send_sem=ask_send.at[j],
            recv_sem=ask_recv.at[j],
            device_id=(along, peer),
            device_id_type=MESH,
        )
        copy.start()
        asks.append(copy)
    own = pltpu.make_async_copy(requests_ref.at[me], asked.at[me], ask_local.at[3])
    own.start()

    for copy in loads[0]:
        copy.wait()

    def fill_table(i, carry):
        for t in range(tiles):
            parts = [
                fields_ref[t, pl.ds(m * cross_dev + i, layers, stride=components * cross_dev), :]
                for m in range(components)
            ]
            rows = jnp.concatenate(parts + [pad], axis=0).T
            table[pl.ds(pl.multiple_of(i * along_dev + t * LANES, LANES), LANES), :] = rows
        return carry

    lax.fori_loop(0, cross_dev, fill_table, 0)

    def fill_weight(source, rows_ref):
        def step(i, carry):
            for t in range(tiles):
                part = source[t, pl.ds(i, layers, stride=cross_dev), :]
                rows = jnp.concatenate([part] * components + [pad], axis=0).T
                rows_ref[pl.ds(pl.multiple_of(i * along_dev + t * LANES, LANES), LANES), :] = rows
            return carry

        lax.fori_loop(0, cross_dev, step, 0)

    locals_ = []
    for j, peer in enumerate(peers):
        asks[j].wait_recv()
        copy = pltpu.make_async_copy(asked_vmem.at[peer], asked.at[peer], ask_local.at[j])
        copy.start()
        locals_.append(copy)
    for copy in locals_ + [own]:
        copy.wait()

    def gather_1(peer, c, dst, base):
        def step(b, carry):
            row = c * (piece // LANES) + b
            start = pl.multiple_of(base + b * LANES, LANES)
            for u in range(LANES):
                dst[pl.ds(start + u, 1), :] = table[pl.ds(asked[peer, row, u], 1), :]
            return carry

        lax.fori_loop(0, piece // LANES, step, 0)

    def gather_2(peer, c, dst, base):
        def step(b, carry):
            row = blocks + c * (piece // LANES) + b
            start = pl.multiple_of(base + b * LANES, LANES)
            for u in range(LANES):
                cell = asked[peer, row, u]
                stage[pl.ds(u, 1), :] = back_1[pl.ds(target_ref[0, cell], 1), :]
                stage_weight[pl.ds(u, 1), :] = first_rows[pl.ds(cell, 1), :]
            dst[pl.ds(start, LANES), :] = blend(stage[...], stage_weight[...], top)
            return carry

        lax.fori_loop(0, piece // LANES, step, 0)

    def exchange(gather, phase, sent, back, beside):
        copies = []
        for c in range(PIECES):
            for j, peer in enumerate(peers[:2]):
                copies.append((j, peer, c))
        for c in range(PIECES):
            copies.append((2, peers[2], c))
        started = []
        waiting = None
        for j, peer, c in copies:
            base = j * capacity + c * piece
            gather(peer, c, sent, base)
            copy = pltpu.make_async_remote_copy(
                src_ref=sent.at[pl.ds(base, piece)],
                dst_ref=back.at[pl.ds(pl.multiple_of(me * capacity + c * piece, LANES), piece)],
                send_sem=send_sem.at[phase, j, c],
                recv_sem=recv_sem.at[phase, j, c],
                device_id=(along, peer),
                device_id_type=MESH,
            )
            if waiting is not None:
                waiting.start()
            waiting = copy
            started.append(copy)
        for c in range(PIECES):
            gather(me, c, back, me * capacity + c * piece)
            if waiting is not None:
                waiting.start()
                waiting = None
        beside()
        for copy in started:
            copy.wait()

    def weights():
        for copy in loads[1] + loads[2]:
            copy.wait()
        fill_weight(first_ref, first_rows)
        fill_weight(second_ref, second_rows)

    exchange(gather_1, 0, sent_1, back_1, weights)
    exchange(gather_2, 1, sent_2, back_2, lambda: None)

    def last(b, carry):
        start = pl.multiple_of(b * LANES, LANES)
        for u in range(LANES):
            final[pl.ds(start + u, 1), :] = back_2[pl.ds(target_ref[1, start + u], 1), :]
        return carry

    lax.fori_loop(0, cells // LANES, last, 0)

    def emit(i, carry):
        for t in range(tiles):
            rows = pl.ds(pl.multiple_of(i * along_dev + t * LANES, LANES), LANES)
            value = blend(final[rows, :], second_rows[rows, :], top).T
            for m in range(components):
                out_ref[
                    t, pl.ds(m * cross_dev + i, layers, stride=components * cross_dev), :
                ] = value[m * layers : (m + 1) * layers]
        return carry

    lax.fori_loop(0, cross_dev, emit, 0)
    stores = [
        pltpu.make_async_copy(
            out_ref.at[t], out_hbm.at[:, pl.ds(t * LANES, LANES)], load_sem.at[3, t]
        )
        for t in range(tiles)
    ]
    for copy in stores:
        copy.start()
    for copy in stores:
        copy.wait()
    for copy in asks:
        copy.wait_send()


def advect_twice(fields, requests, target, first_fraction, second_fraction):
    layers, components, cross_dev, along_dev = fields.shape
    cells = cross_dev * along_dev
    partners, substeps, capacity = requests.shape
    width = (layers * components + LANES - 1) // LANES * LANES
    vmem = pl.BlockSpec(memory_space=pltpu.VMEM)
    smem = pl.BlockSpec(memory_space=pltpu.SMEM)
    hbm = pl.BlockSpec(memory_space=pl.ANY)
    tiles = along_dev // LANES
    grid = requests.reshape(partners, substeps * capacity // LANES, LANES)
    rows = lambda count: pltpu.VMEM((count, width), jnp.float32)
    moved = pl.pallas_call(
        functools.partial(exchange_kernel, layers, components, cross_dev, capacity),
        out_shape=jax.ShapeDtypeStruct((layers * components * cross_dev, along_dev), jnp.float32),
        in_specs=[smem, vmem, hbm, hbm, hbm],
        out_specs=hbm,
        scratch_shapes=[
            pltpu.VMEM((tiles, layers * components * cross_dev, LANES), jnp.float32),
            pltpu.VMEM((tiles, layers * cross_dev, LANES), jnp.float32),
            pltpu.VMEM((tiles, layers * cross_dev, LANES), jnp.float32),
            pltpu.VMEM((tiles, layers * components * cross_dev, LANES), jnp.float32),
            pltpu.VMEM(grid.shape, jnp.int32),
            pltpu.SMEM(grid.shape, jnp.int32),
            rows(cells),
            rows(cells),
            rows(cells),
            rows(3 * capacity),
            rows(3 * capacity),
            rows(4 * capacity),
            rows(4 * capacity),
            rows(LANES),
            rows(LANES),
            rows(cells),
            pltpu.SemaphoreType.DMA((3,)),
            pltpu.SemaphoreType.DMA((3,)),
            pltpu.SemaphoreType.DMA((4,)),
            pltpu.SemaphoreType.DMA((2, 3, PIECES)),
            pltpu.SemaphoreType.DMA((2, 3, PIECES)),
            pltpu.SemaphoreType.DMA((4, tiles)),
        ],
        compiler_params=pltpu.CompilerParams(collective_id=0, has_side_effects=True),
        name="advect_twice",
    )(
        target,
        grid,
        fields.reshape(layers * components * cross_dev, along_dev),
        first_fraction.reshape(layers * cross_dev, along_dev),
        second_fraction.reshape(layers * cross_dev, along_dev),
    )
    return moved.reshape(fields.shape)


def body(
    fields,
    first_feet,
    first_fraction,
    second_feet,
    second_fraction,
    lateral_mix,
    vertical_mix,
    bottom_drag,
    surface_stress,
):
    layers, components, cross_dev, along_dev = fields.shape
    cells = cross_dev * along_dev
    row_count = layers * components
    width = (row_count + 127) // 128 * 128

    requests, target = plan(jnp.stack([first_feet, second_feet]), cross_dev, along_dev)
    across_count, span, substeps, capacity = requests.shape

    if span == 1 and across_count == 4 and capacity % (PIECES * LANES) == 0:
        moved = advect_twice(fields, requests[:, 0], target, first_fraction, second_fraction)
    else:
        asked = to_holders(requests.reshape(across_count, span, substeps * capacity))

        def advect(table, asked, target, fraction):
            weight = jnp.pad(
                jnp.tile(fraction.reshape(layers, cells), (components, 1)),
                ((0, width - row_count), (0, 0)),
            ).T
            picked = gather_rows(table, asked.reshape(-1))
            returned = to_askers(picked.reshape(asked.shape + (width,)))
            return blend_rows(returned.reshape(-1, width), target, weight, layers)

        table = fields.transpose(1, 0, 2, 3).reshape(row_count, cells)
        table = jnp.pad(table, ((0, width - row_count), (0, 0))).T
        middle = advect(table, asked[:, :, :capacity], target[0], first_fraction)
        moved = advect(middle, asked[:, :, capacity:], target[1], second_fraction)
        moved = moved.T[:row_count].reshape(components, layers, cross_dev, along_dev)
        moved = moved.transpose(1, 0, 2, 3)
    padded = padded_2(moved, (("across", 2), ("along", 3)), 1)
    beside_all = neighbour_sum(padded)
    row_total = cross_dev * lax.axis_size("across")
    column_total = along_dev * lax.axis_size("along")
    row_index = lax.axis_index("across") * cross_dev + jnp.arange(cross_dev, dtype=jnp.int32)
    column_index = lax.axis_index("along") * along_dev + jnp.arange(along_dev, dtype=jnp.int32)
    row_present = (row_index > 0).astype(jnp.float32) + (row_index < row_total - 1).astype(
        jnp.float32
    )
    column_present = (column_index > 0).astype(jnp.float32) + (
        column_index < column_total - 1
    ).astype(jnp.float32)
    present = row_present[:, None] + column_present[None, :]
    mixed = moved + lateral_mix * (beside_all - present * moved)
    return solve_columns(mixed, vertical_mix, bottom_drag, surface_stress)


def solution(mesh):
    in_specs = (
        P(None, None, "across", "along"),
        P("across", "along"),
        P(None, "across", "along"),
        P("across", "along"),
        P(None, "across", "along"),
        P("across", "along"),
        P(None, None, "across", "along"),
        P("across", "along"),
        P(None, "across", "along"),
    )
    out_specs = P(None, None, "across", "along")
    return jax.shard_map(body, mesh=mesh, in_specs=in_specs, out_specs=out_specs, check_vma=False)
```

```python
import functools

import jax
import jax.numpy as jnp
from jax import lax
from jax.experimental import pallas as pl
from jax.experimental.pallas import tpu as pltpu
from jax.sharding import PartitionSpec as P


def shifted(block, axis, distance):
    devices = range(lax.axis_size(axis))
    route = [(i - distance, i) for i in devices if i - distance in devices]
    return lax.ppermute(block, axis, route)


def padded_2(value, sides, width):
    for axis, dim in sides:
        count, length = (lax.axis_size(axis), value.shape[dim])
        up = [(i, (i + 1) % count) for i in range(count - 1)]
        down = [(j, i) for i, j in up]
        last = lax.slice_in_dim(value, length - width, length, axis=dim)
        first = lax.slice_in_dim(value, 0, width, axis=dim)
        before = lax.ppermute(last, axis, up)
        after = lax.ppermute(first, axis, down)
        value = jnp.concatenate([before, value, after], axis=dim)
    return value


def neighbour_sum(padded):
    total = padded[:, :, :-2, 1:-1] + padded[:, :, 2:, 1:-1]
    return total + padded[:, :, 1:-1, :-2] + padded[:, :, 1:-1, 2:]


def solve_columns(forcing, vertical_mix, bottom_drag, surface_stress):
    layers = forcing.shape[0]
    coupling = jnp.stack([vertical_mix[0], vertical_mix[0], vertical_mix[1]], axis=1)
    nothing = jnp.zeros_like(coupling[:1])
    below = jnp.concatenate([nothing, coupling], axis=0)
    above = jnp.concatenate([coupling, nothing], axis=0)
    friction = jnp.stack([bottom_drag, bottom_drag, jnp.zeros_like(bottom_drag)], axis=0)
    diagonal = (1.0 + below + above).at[0].add(friction)
    source = forcing.at[layers - 1, 0:2].add(surface_stress)
    factor = above[0] / diagonal[0]
    partial_value = source[0] / diagonal[0]
    factors = [factor]
    partials = [partial_value]
    for level_index in range(1, layers):
        denominator = diagonal[level_index] - below[level_index] * factor
        factor = above[level_index] / denominator
        partial_value = (source[level_index] + below[level_index] * partial_value) / denominator
        factors.append(factor)
        partials.append(partial_value)
    solution = partials[layers - 1]
    results = [solution]
    for level_index in range(layers - 2, -1, -1):
        solution = partials[level_index] + factors[level_index] * solution
        results.append(solution)
    return jnp.stack(results[::-1], axis=0)


def owners(feet, cross_dev, along_dev, along_total):
    flat_feet = feet
    global_row = flat_feet // along_total
    global_column = flat_feet % along_total
    local_cell = global_row % cross_dev * along_dev + global_column % along_dev
    return (global_column // along_dev, global_row // cross_dev, local_cell)


def prefix_count(member):
    partners, cells = member.shape
    lanes = 128
    blocks = member.reshape(partners, cells // lanes, lanes)
    before = jnp.triu(jnp.ones((lanes, lanes), jnp.bfloat16), 1)
    inside = lax.dot_general(
        blocks.astype(jnp.bfloat16), before, (((2,), (0,)), ((), ())),
        preferred_element_type=jnp.float32,
    ).astype(jnp.int32)
    totals = blocks.sum(axis=2)
    ahead = jnp.cumsum(totals, axis=1) - totals
    return (inside + ahead[:, :, None]).reshape(partners, cells), totals.sum(axis=1)


def plan(feet, cross_dev, along_dev):
    along_count = lax.axis_size("along")
    across_count = lax.axis_size("across")
    cells = cross_dev * along_dev
    reach = along_count // 8
    capacity = 9 * cells // (8 * across_count * reach)
    span = 2 * reach - 1
    partners = across_count * span
    substeps = feet.shape[0]
    owner_along, owner_across, local_cell = owners(
        feet.reshape(substeps, cells), cross_dev, along_dev, along_dev * along_count
    )
    offset = owner_along - lax.axis_index("along")
    partner = owner_across * span + offset + reach - 1
    key = (partner * cells + jnp.arange(cells, dtype=jnp.int32)) * cells + local_cell
    ordered = [jnp.pad(lax.sort(key[s]) % cells, (0, capacity)) for s in range(substeps)]
    labels = jnp.arange(partners, dtype=jnp.int32)[:, None]
    member = (partner[:, None, :] == labels).astype(jnp.int32)
    rank, counts = prefix_count(member.reshape(substeps * partners, cells))
    rank = rank.reshape(substeps, partners, cells)
    target = jnp.sum(member * (rank + capacity * labels), axis=1)
    counts = counts.reshape(substeps, partners)
    starts = jnp.cumsum(counts, axis=1) - counts
    requests = [
        lax.dynamic_slice(ordered[s], (starts[s, p],), (capacity,))
        for p in range(partners)
        for s in range(substeps)
    ]
    return jnp.stack(requests).reshape(across_count, span, substeps, capacity), target


def hop_groups(reach, power):
    upward = [offset + reach - 1 for offset in range(1 - reach, 0) if -offset >> power & 1]
    downward = [offset + reach - 1 for offset in range(1, reach) if offset >> power & 1]
    return (upward, downward)


UNROLL = 32


def gather_kernel(index_ref, table_ref, out_ref):
    def step(i, carry):
        base = pl.multiple_of(i * UNROLL, UNROLL)
        for u in range(UNROLL):
            out_ref[pl.ds(base + u, 1), :] = table_ref[pl.ds(index_ref[base + u], 1), :]
        return carry

    lax.fori_loop(0, out_ref.shape[0] // UNROLL, step, 0)


def gather_rows(table, index):
    count, width = index.shape[0], table.shape[1]
    return pl.pallas_call(
        gather_kernel,
        out_shape=jax.ShapeDtypeStruct((count, width), table.dtype),
        in_specs=[
            pl.BlockSpec(memory_space=pltpu.SMEM),
            pl.BlockSpec(memory_space=pltpu.VMEM),
        ],
        out_specs=pl.BlockSpec(memory_space=pltpu.VMEM),
        name="gather_rows",
    )(index, table)


def blend_kernel(layers, index_ref, table_ref, fraction_ref, out_ref):
    width = out_ref.shape[1]
    lane = lax.broadcasted_iota(jnp.int32, (UNROLL, width), 1)
    top = lane % layers == layers - 1

    def step(i, carry):
        base = pl.multiple_of(i * UNROLL, UNROLL)
        for u in range(UNROLL):
            out_ref[pl.ds(base + u, 1), :] = table_ref[pl.ds(index_ref[base + u], 1), :]
        rows = out_ref[pl.ds(base, UNROLL), :]
        upper = jnp.where(top, rows, pltpu.roll(rows, width - 1, 1))
        weight = fraction_ref[pl.ds(base, UNROLL), :]
        out_ref[pl.ds(base, UNROLL), :] = (1.0 - weight) * rows + weight * upper
        return carry

    lax.fori_loop(0, out_ref.shape[0] // UNROLL, step, 0)


def blend_rows(table, index, fraction, layers):
    return pl.pallas_call(
        functools.partial(blend_kernel, layers),
        out_shape=jax.ShapeDtypeStruct(fraction.shape, table.dtype),
        in_specs=[
            pl.BlockSpec(memory_space=pltpu.SMEM),
            pl.BlockSpec(memory_space=pltpu.VMEM),
            pl.BlockSpec(memory_space=pltpu.VMEM),
        ],
        out_specs=pl.BlockSpec(memory_space=pltpu.VMEM),
        name="blend_rows",
    )(index, table, fraction)


def to_holders(requests):
    reach = (requests.shape[1] + 1) // 2
    moved = lax.all_to_all(requests, "across", split_axis=0, concat_axis=0, tiled=True)
    for power in range((reach - 1).bit_length()):
        upward, downward = hop_groups(reach, power)
        moved = moved.at[:, upward].set(shifted(moved[:, upward], "along", -(1 << power)))
        moved = moved.at[:, downward].set(shifted(moved[:, downward], "along", 1 << power))
    return moved


def to_askers(picked):
    reach = (picked.shape[1] + 1) // 2
    for power in range((reach - 1).bit_length()):
        upward, downward = hop_groups(reach, power)
        picked = picked.at[:, upward].set(shifted(picked[:, upward], "along", 1 << power))
        picked = picked.at[:, downward].set(shifted(picked[:, downward], "along", -(1 << power)))
    return lax.all_to_all(picked, "across", split_axis=0, concat_axis=0, tiled=True)


LANES = 128
PIECES = 3
MESH = pl.DeviceIdType.MESH


def blend(rows, weight, top):
    upper = jnp.where(top, rows, pltpu.roll(rows, rows.shape[1] - 1, 1))
    return (1.0 - weight) * rows + weight * upper


def exchange_kernel(
    layers,
    components,
    cross_dev,
    capacity,
    target_ref,
    requests_ref,
    fields_hbm,
    first_hbm,
    second_hbm,
    out_ref,
    west_ref,
    east_ref,
    north_ref,
    south_ref,
    fields_ref,
    first_ref,
    second_ref,
    asked_vmem,
    asked,
    table,
    first_rows,
    second_rows,
    sent_1,
    sent_2,
    back_1,
    back_2,
    stage,
    stage_weight,
    final,
    ask_send,
    ask_recv,
    ask_local,
    send_sem,
    recv_sem,
    load_sem,
    edge_w,
    edge_e,
    halo_n,
    halo_s,
    halo_w,
    halo_e,
    halo_send,
    halo_recv,
):
    tiles = fields_ref.shape[0]
    along_dev = tiles * LANES
    cells = cross_dev * along_dev
    width = table.shape[1]
    blocks = capacity // LANES
    piece = capacity // PIECES
    along = lax.axis_index("along")
    me = lax.axis_index("across")
    peers = [lax.rem(me + 2, 4), 3 - me, me + 1 - 2 * lax.rem(me, 2)]
    pad = jnp.zeros((width - layers * components, LANES), jnp.float32)
    top = lax.broadcasted_iota(jnp.int32, (LANES, width), 1) % layers == layers - 1

    loads = [
        [
            pltpu.make_async_copy(
                source.at[:, pl.ds(t * LANES, LANES)], place.at[t], load_sem.at[s, t]
            )
            for t in range(tiles)
        ]
        for s, (source, place) in enumerate(
            [(fields_hbm, fields_ref), (first_hbm, first_ref), (second_hbm, second_ref)]
        )
    ]
    for group in loads:
        for copy in group:
            copy.start()

    barrier = pltpu.get_barrier_semaphore()
    for peer in peers:
        pl.semaphore_signal(barrier, inc=1, device_id=(along, peer), device_id_type=MESH)
    along_count = lax.axis_size("along")
    has_west, has_east = along > 0, along < along_count - 1
    has_north, has_south = me > 0, me < lax.axis_size("across") - 1

    @pl.when(has_west)
    def _():
        pl.semaphore_signal(barrier, inc=1, device_id=(along - 1, me), device_id_type=MESH)

    @pl.when(has_east)
    def _():
        pl.semaphore_signal(barrier, inc=1, device_id=(along + 1, me), device_id_type=MESH)

    pl.semaphore_wait(barrier, 3 + has_west.astype(jnp.int32) + has_east.astype(jnp.int32))

    asks = []
    for j, peer in enumerate(peers):
        copy = pltpu.make_async_remote_copy(
            src_ref=requests_ref.at[peer],
            dst_ref=asked_vmem.at[me],
            send_sem=ask_send.at[j],
            recv_sem=ask_recv.at[j],
            device_id=(along, peer),
            device_id_type=MESH,
        )
        copy.start()
        asks.append(copy)
    own = pltpu.make_async_copy(requests_ref.at[me], asked.at[me], ask_local.at[3])
    own.start()

    for copy in loads[0]:
        copy.wait()

    def fill_table(i, carry):
        for t in range(tiles):
            parts = [
                fields_ref[t, pl.ds(m * cross_dev + i, layers, stride=components * cross_dev), :]
                for m in range(components)
            ]
            rows = jnp.concatenate(parts + [pad], axis=0).T
            table[pl.ds(pl.multiple_of(i * along_dev + t * LANES, LANES), LANES), :] = rows
        return carry

    lax.fori_loop(0, cross_dev, fill_table, 0)

    def fill_weight(source, rows_ref):
        def step(i, carry):
            for t in range(tiles):
                part = source[t, pl.ds(i, layers, stride=cross_dev), :]
                rows = jnp.concatenate([part] * components + [pad], axis=0).T
                rows_ref[pl.ds(pl.multiple_of(i * along_dev + t * LANES, LANES), LANES), :] = rows
            return carry

        lax.fori_loop(0, cross_dev, step, 0)

    locals_ = []
    for j, peer in enumerate(peers):
        asks[j].wait_recv()
        copy = pltpu.make_async_copy(asked_vmem.at[peer], asked.at[peer], ask_local.at[j])
        copy.start()
        locals_.append(copy)
    for copy in locals_ + [own]:
        copy.wait()

    def gather_1(peer, c, dst, base):
        def step(b, carry):
            row = c * (piece // LANES) + b
            start = pl.multiple_of(base + b * LANES, LANES)
            for u in range(LANES):
                dst[pl.ds(start + u, 1), :] = table[pl.ds(asked[peer, row, u], 1), :]
            return carry

        lax.fori_loop(0, piece // LANES, step, 0)

    def gather_2(peer, c, dst, base):
        def step(b, carry):
            row = blocks + c * (piece // LANES) + b
            start = pl.multiple_of(base + b * LANES, LANES)
            for u in range(LANES):
                cell = asked[peer, row, u]
                stage[pl.ds(u, 1), :] = back_1[pl.ds(target_ref[0, cell], 1), :]
                stage_weight[pl.ds(u, 1), :] = first_rows[pl.ds(cell, 1), :]
            dst[pl.ds(start, LANES), :] = blend(stage[...], stage_weight[...], top)
            return carry

        lax.fori_loop(0, piece // LANES, step, 0)

    def exchange(gather, phase, sent, back, beside):
        copies = []
        for c in range(PIECES):
            for j, peer in enumerate(peers[:2]):
                copies.append((j, peer, c))
        for c in range(PIECES):
            copies.append((2, peers[2], c))
        started = []
        waiting = None
        for j, peer, c in copies:
            base = j * capacity + c * piece
            gather(peer, c, sent, base)
            copy = pltpu.make_async_remote_copy(
                src_ref=sent.at[pl.ds(base, piece)],
                dst_ref=back.at[pl.ds(pl.multiple_of(me * capacity + c * piece, LANES), piece)],
                send_sem=send_sem.at[phase, j, c],
                recv_sem=recv_sem.at[phase, j, c],
                device_id=(along, peer),
                device_id_type=MESH,
            )
            if waiting is not None:
                waiting.start()
            waiting = copy
            started.append(copy)
        for c in range(PIECES):
            gather(me, c, back, me * capacity + c * piece)
            if waiting is not None:
                waiting.start()
                waiting = None
        beside()
        for copy in started:
            copy.wait()

    def weights():
        for copy in loads[1] + loads[2]:
            copy.wait()
        fill_weight(first_ref, first_rows)
        fill_weight(second_ref, second_rows)

    exchange(gather_1, 0, sent_1, back_1, weights)
    exchange(gather_2, 1, sent_2, back_2, lambda: None)

    def unpack(start):
        start = pl.multiple_of(start, LANES)
        for u in range(LANES):
            final[pl.ds(start + u, 1), :] = back_2[pl.ds(target_ref[1, start + u], 1), :]
        rows = pl.ds(start, LANES)
        final[rows, :] = blend(final[rows, :], second_rows[rows, :], top)

    def unpack_row(first):
        def step(t, carry):
            unpack(first + t * LANES)
            return carry

        lax.fori_loop(0, tiles, step, 0)

    def halo(j, source, place, peer):
        return pltpu.make_async_remote_copy(
            src_ref=source,
            dst_ref=place,
            send_sem=halo_send.at[j],
            recv_sem=halo_recv.at[j],
            device_id=peer,
            device_id_type=MESH,
        )

    top_row, last_row = pl.ds(0, along_dev), pl.ds(cells - along_dev, along_dev)
    north = halo(0, final.at[top_row], halo_s, (along, me - 1))
    south = halo(1, final.at[last_row], halo_n, (along, me + 1))
    west = halo(2, edge_w, halo_e, (along - 1, me))
    east = halo(3, edge_e, halo_w, (along + 1, me))

    unpack_row(0)
    unpack_row(cells - along_dev)
    inner = cross_dev - 2

    def outer_columns(i, carry):
        unpack((i + 1) * along_dev)
        unpack((i + 2) * along_dev - LANES)
        return carry

    lax.fori_loop(0, inner, outer_columns, 0)

    for i in range(cross_dev):
        edge_w[pl.ds(i, 1), :] = final[pl.ds(i * along_dev, 1), :]
        edge_e[pl.ds(i, 1), :] = final[pl.ds((i + 1) * along_dev - 1, 1), :]

    for present, copy in [
        (has_north, north), (has_south, south), (has_west, west), (has_east, east)
    ]:
        @pl.when(present)
        def _(copy=copy):
            copy.start()

    def inner_columns(i, carry):
        def step(t, carry):
            unpack((i + 1) * along_dev + (t + 1) * LANES)
            return carry

        return lax.fori_loop(0, tiles - 2, step, carry)

    lax.fori_loop(0, inner, inner_columns, 0)

    def spread(value, ref, first, stride, t):
        for m in range(components):
            ref[t, pl.ds(m * stride + first, layers, stride=components * stride), :] = value[
                m * layers : (m + 1) * layers
            ]

    def emit(i, carry):
        for t in range(tiles):
            rows = pl.ds(pl.multiple_of(i * along_dev + t * LANES, LANES), LANES)
            spread(final[rows, :].T, out_ref, i, cross_dev, t)
        return carry

    lax.fori_loop(0, cross_dev, emit, 0)

    for present, copy, place in [
        (has_south, north, halo_s),
        (has_north, south, halo_n),
        (has_east, west, halo_e),
        (has_west, east, halo_w),
    ]:
        @pl.when(present)
        def _(copy=copy):
            copy.wait_recv()

        @pl.when(jnp.logical_not(present))
        def _(place=place):
            place[...] = jnp.zeros_like(place)

    for t in range(tiles):
        rows = pl.ds(t * LANES, LANES)
        spread(halo_n[rows, :].T, north_ref, 0, 1, t)
        spread(halo_s[rows, :].T, south_ref, 0, 1, t)
    for i in range(cross_dev):
        for source, place in [(halo_w, west_ref), (halo_e, east_ref)]:
            row = jnp.broadcast_to(source[pl.ds(i, 1), :], (LANES, width))
            spread(row.T, place, i, cross_dev, 0)

    for present, copy in [
        (has_north, north), (has_south, south), (has_west, west), (has_east, east)
    ]:
        @pl.when(present)
        def _(copy=copy):
            copy.wait_send()

    for copy in asks:
        copy.wait_send()


def advect_twice(fields, requests, target, first_fraction, second_fraction):
    layers, components, cross_dev, along_dev = fields.shape
    cells = cross_dev * along_dev
    partners, substeps, capacity = requests.shape
    width = (layers * components + LANES - 1) // LANES * LANES
    vmem = pl.BlockSpec(memory_space=pltpu.VMEM)
    smem = pl.BlockSpec(memory_space=pltpu.SMEM)
    hbm = pl.BlockSpec(memory_space=pl.ANY)
    tiles = along_dev // LANES
    grid = requests.reshape(partners, substeps * capacity // LANES, LANES)
    rows = lambda count: pltpu.VMEM((count, width), jnp.float32)
    shape = lambda *dims: jax.ShapeDtypeStruct(dims, jnp.float32)
    edge = layers * components
    return pl.pallas_call(
        functools.partial(exchange_kernel, layers, components, cross_dev, capacity),
        out_shape=[
            shape(tiles, edge * cross_dev, LANES),
            shape(1, edge * cross_dev, LANES),
            shape(1, edge * cross_dev, LANES),
            shape(tiles, edge, LANES),
            shape(tiles, edge, LANES),
        ],
        in_specs=[smem, vmem, hbm, hbm, hbm],
        out_specs=[vmem] * 5,
        scratch_shapes=[
            pltpu.VMEM((tiles, layers * components * cross_dev, LANES), jnp.float32),
            pltpu.VMEM((tiles, layers * cross_dev, LANES), jnp.float32),
            pltpu.VMEM((tiles, layers * cross_dev, LANES), jnp.float32),
            pltpu.VMEM(grid.shape, jnp.int32),
            pltpu.SMEM(grid.shape, jnp.int32),
            rows(cells),
            rows(cells),
            rows(cells),
            rows(3 * capacity),
            rows(3 * capacity),
            rows(4 * capacity),
            rows(4 * capacity),
            rows(LANES),
            rows(LANES),
            rows(cells),
            pltpu.SemaphoreType.DMA((3,)),
            pltpu.SemaphoreType.DMA((3,)),
            pltpu.SemaphoreType.DMA((4,)),
            pltpu.SemaphoreType.DMA((2, 3, PIECES)),
            pltpu.SemaphoreType.DMA((2, 3, PIECES)),
            pltpu.SemaphoreType.DMA((3, tiles)),
            rows(cross_dev),
            rows(cross_dev),
            rows(along_dev),
            rows(along_dev),
            rows(cross_dev),
            rows(cross_dev),
            pltpu.SemaphoreType.DMA((4,)),
            pltpu.SemaphoreType.DMA((4,)),
        ],
        compiler_params=pltpu.CompilerParams(collective_id=0, has_side_effects=True),
        name="advect_twice",
    )(
        target,
        grid,
        fields.reshape(layers * components * cross_dev, along_dev),
        first_fraction.reshape(layers * cross_dev, along_dev),
        second_fraction.reshape(layers * cross_dev, along_dev),
    )


def solve_kernel(
    layers,
    components,
    moved_ref,
    west_ref,
    east_ref,
    north_ref,
    south_ref,
    present_ref,
    lateral_ref,
    mix_ref,
    drag_ref,
    stress_ref,
    out_ref,
    factors,
):
    cross_dev = out_ref.shape[2]
    tiles = moved_ref.shape[0]
    lane = lax.broadcasted_iota(jnp.int32, (cross_dev, LANES), 1)
    row = lax.broadcasted_iota(jnp.int32, (cross_dev, LANES), 0)
    at = [pl.ds(t * LANES, LANES) for t in range(tiles)]
    lateral = [lateral_ref[:, at[t]] for t in range(tiles)]
    present = [present_ref[:, at[t]] for t in range(tiles)]

    def mixed(k, m):
        level = k * components + m
        rows = pl.ds(pl.multiple_of(level * cross_dev, cross_dev), cross_dev)
        here = [moved_ref[t, rows, :] for t in range(tiles)]
        right = [pltpu.roll(x, 1, 1) for x in [west_ref[0, rows, :]] + here]
        left = [pltpu.roll(x, LANES - 1, 1) for x in here + [east_ref[0, rows, :]]]
        result = []
        for t in range(tiles):
            x = here[t]
            before = jnp.where(lane == 0, right[t], right[t + 1])
            after = jnp.where(lane == LANES - 1, left[t + 1], left[t])
            above = jnp.where(
                row == 0, north_ref[t, pl.ds(level, 1), :], pltpu.roll(x, 1, 0)
            )
            below = jnp.where(
                row == cross_dev - 1,
                south_ref[t, pl.ds(level, 1), :],
                pltpu.roll(x, cross_dev - 1, 0),
            )
            total = above + below + before + after
            result.append(x + lateral[t] * (total - present[t] * x))
        return result

    def forward(k, carry, first=False, final=False):
        factor, partial = carry or (None, None)
        source = [mixed(k, m) for m in range(components)]
        new_factor, new_partial = [], [None] * components
        for g in range(2):
            members = (0, 1) if g == 0 else (2,)
            row_factor = []
            for t in range(tiles):
                above = 0.0 if final else mix_ref[g, k, :, at[t]]
                below = 0.0 if first else mix_ref[g, k - 1, :, at[t]]
                diagonal = 1.0 + below + above
                if first:
                    if g == 0:
                        diagonal = diagonal + drag_ref[:, at[t]]
                else:
                    diagonal = diagonal - below * factor[g][t]
                inverse = 1.0 / diagonal
                for m in members:
                    value = source[m][t]
                    if final and g == 0:
                        value = value + stress_ref[m, :, at[t]]
                    if not first:
                        value = value + below * partial[m][t]
                    value = value * inverse
                    new_partial[m] = (new_partial[m] or []) + [value]
                    out_ref[k, m, :, at[t]] = value
                if not final:
                    ratio = above * inverse
                    factors[g, k, :, at[t]] = ratio
                    row_factor.append(ratio)
            new_factor.append(row_factor)
        return new_factor, new_partial

    carry = forward(0, None, first=True)
    carry = lax.fori_loop(1, layers - 1, forward, carry)
    _, value = forward(layers - 1, carry, final=True)

    def backward(step, value):
        k = layers - 2 - step
        result = []
        for m in range(components):
            g = 0 if m < 2 else 1
            level = []
            for t in range(tiles):
                x = out_ref[k, m, :, at[t]] + factors[g, k, :, at[t]] * value[m][t]
                out_ref[k, m, :, at[t]] = x
                level.append(x)
            result.append(level)
        return result

    lax.fori_loop(0, layers - 1, backward, value)


def mix_and_solve(pieces, present, lateral_mix, vertical_mix, bottom_drag, surface_stress, shape):
    layers, components, cross_dev, along_dev = shape
    vmem = pl.BlockSpec(memory_space=pltpu.VMEM)
    return pl.pallas_call(
        functools.partial(solve_kernel, layers, components),
        out_shape=jax.ShapeDtypeStruct(shape, jnp.float32),
        in_specs=[vmem] * 10,
        out_specs=vmem,
        scratch_shapes=[pltpu.VMEM((2, layers - 1, cross_dev, along_dev), jnp.float32)],
        name="mix_and_solve",
    )(*pieces, present, lateral_mix, vertical_mix, bottom_drag, surface_stress)


def body(
    fields,
    first_feet,
    first_fraction,
    second_feet,
    second_fraction,
    lateral_mix,
    vertical_mix,
    bottom_drag,
    surface_stress,
):
    layers, components, cross_dev, along_dev = fields.shape
    cells = cross_dev * along_dev
    row_count = layers * components
    width = (row_count + 127) // 128 * 128

    requests, target = plan(jnp.stack([first_feet, second_feet]), cross_dev, along_dev)
    across_count, span, substeps, capacity = requests.shape

    row_total = cross_dev * lax.axis_size("across")
    column_total = along_dev * lax.axis_size("along")
    row_index = lax.axis_index("across") * cross_dev + jnp.arange(cross_dev, dtype=jnp.int32)
    column_index = lax.axis_index("along") * along_dev + jnp.arange(along_dev, dtype=jnp.int32)
    row_present = (row_index > 0).astype(jnp.float32) + (row_index < row_total - 1).astype(
        jnp.float32
    )
    column_present = (column_index > 0).astype(jnp.float32) + (
        column_index < column_total - 1
    ).astype(jnp.float32)
    present = row_present[:, None] + column_present[None, :]
    if span == 1 and across_count == 4 and capacity % (PIECES * LANES) == 0:
        pieces = advect_twice(fields, requests[:, 0], target, first_fraction, second_fraction)
        return mix_and_solve(
            pieces,
            present,
            lateral_mix,
            vertical_mix,
            bottom_drag,
            surface_stress,
            fields.shape,
        )
    else:
        asked = to_holders(requests.reshape(across_count, span, substeps * capacity))

        def advect(table, asked, target, fraction):
            weight = jnp.pad(
                jnp.tile(fraction.reshape(layers, cells), (components, 1)),
                ((0, width - row_count), (0, 0)),
            ).T
            picked = gather_rows(table, asked.reshape(-1))
            returned = to_askers(picked.reshape(asked.shape + (width,)))
            return blend_rows(returned.reshape(-1, width), target, weight, layers)

        table = fields.transpose(1, 0, 2, 3).reshape(row_count, cells)
        table = jnp.pad(table, ((0, width - row_count), (0, 0))).T
        middle = advect(table, asked[:, :, :capacity], target[0], first_fraction)
        moved = advect(middle, asked[:, :, capacity:], target[1], second_fraction)
        moved = moved.T[:row_count].reshape(components, layers, cross_dev, along_dev)
        moved = moved.transpose(1, 0, 2, 3)
    padded = padded_2(moved, (("across", 2), ("along", 3)), 1)
    beside_all = neighbour_sum(padded)
    mixed = moved + lateral_mix * (beside_all - present * moved)
    return solve_columns(mixed, vertical_mix, bottom_drag, surface_stress)


def solution(mesh):
    in_specs = (
        P(None, None, "across", "along"),
        P("across", "along"),
        P(None, "across", "along"),
        P("across", "along"),
        P(None, "across", "along"),
        P("across", "along"),
        P(None, None, "across", "along"),
        P("across", "along"),
        P(None, "across", "along"),
    )
    out_specs = P(None, None, "across", "along")
    return jax.shard_map(body, mesh=mesh, in_specs=in_specs, out_specs=out_specs, check_vma=False)
```

```python
import functools

import jax
import jax.numpy as jnp
from jax import lax
from jax.experimental import pallas as pl
from jax.experimental.pallas import tpu as pltpu
from jax.sharding import PartitionSpec as P


def shifted(block, axis, distance):
    devices = range(lax.axis_size(axis))
    route = [(i - distance, i) for i in devices if i - distance in devices]
    return lax.ppermute(block, axis, route)


def padded_2(value, sides, width):
    for axis, dim in sides:
        count, length = (lax.axis_size(axis), value.shape[dim])
        up = [(i, (i + 1) % count) for i in range(count - 1)]
        down = [(j, i) for i, j in up]
        last = lax.slice_in_dim(value, length - width, length, axis=dim)
        first = lax.slice_in_dim(value, 0, width, axis=dim)
        before = lax.ppermute(last, axis, up)
        after = lax.ppermute(first, axis, down)
        value = jnp.concatenate([before, value, after], axis=dim)
    return value


def neighbour_sum(padded):
    total = padded[:, :, :-2, 1:-1] + padded[:, :, 2:, 1:-1]
    return total + padded[:, :, 1:-1, :-2] + padded[:, :, 1:-1, 2:]


def solve_columns(forcing, vertical_mix, bottom_drag, surface_stress):
    layers = forcing.shape[0]
    coupling = jnp.stack([vertical_mix[0], vertical_mix[0], vertical_mix[1]], axis=1)
    nothing = jnp.zeros_like(coupling[:1])
    below = jnp.concatenate([nothing, coupling], axis=0)
    above = jnp.concatenate([coupling, nothing], axis=0)
    friction = jnp.stack([bottom_drag, bottom_drag, jnp.zeros_like(bottom_drag)], axis=0)
    diagonal = (1.0 + below + above).at[0].add(friction)
    source = forcing.at[layers - 1, 0:2].add(surface_stress)
    factor = above[0] / diagonal[0]
    partial_value = source[0] / diagonal[0]
    factors = [factor]
    partials = [partial_value]
    for level_index in range(1, layers):
        denominator = diagonal[level_index] - below[level_index] * factor
        factor = above[level_index] / denominator
        partial_value = (source[level_index] + below[level_index] * partial_value) / denominator
        factors.append(factor)
        partials.append(partial_value)
    solution = partials[layers - 1]
    results = [solution]
    for level_index in range(layers - 2, -1, -1):
        solution = partials[level_index] + factors[level_index] * solution
        results.append(solution)
    return jnp.stack(results[::-1], axis=0)


def owners(feet, cross_dev, along_dev, along_total):
    flat_feet = feet
    global_row = flat_feet // along_total
    global_column = flat_feet % along_total
    local_cell = global_row % cross_dev * along_dev + global_column % along_dev
    return (global_column // along_dev, global_row // cross_dev, local_cell)


def prefix_count(member):
    partners, cells = member.shape
    lanes = 128
    blocks = member.reshape(partners, cells // lanes, lanes)
    before = jnp.triu(jnp.ones((lanes, lanes), jnp.bfloat16), 1)
    inside = lax.dot_general(
        blocks.astype(jnp.bfloat16), before, (((2,), (0,)), ((), ())),
        preferred_element_type=jnp.float32,
    ).astype(jnp.int32)
    totals = blocks.sum(axis=2)
    ahead = jnp.cumsum(totals, axis=1) - totals
    return (inside + ahead[:, :, None]).reshape(partners, cells), totals.sum(axis=1)


LANES = 128


def cut_kernel(capacity, starts_ref, ordered_ref, out_ref):
    partners, substeps = out_ref.shape[:2]
    blocks = capacity // LANES
    lane = lax.broadcasted_iota(jnp.int32, (blocks, LANES), 1)
    for p in range(partners):
        for s in range(substeps):
            start = starts_ref[s, p]
            first = start // LANES
            shift = start - first * LANES
            rows = ordered_ref[s, pl.ds(first, blocks + 7), :]
            turned = pltpu.roll(rows, lax.rem(LANES - shift, LANES), 1)
            out_ref[p, s] = jnp.where(
                lane < LANES - shift, turned[:blocks], turned[1 : blocks + 1]
            )


def cut_requests(ordered, starts, capacity):
    substeps, length = ordered.shape
    rows = (length + 8 * LANES - 1) // LANES + 7
    ordered = jnp.pad(ordered, ((0, 0), (0, rows * LANES - length)))
    vmem = pl.BlockSpec(memory_space=pltpu.VMEM)
    return pl.pallas_call(
        functools.partial(cut_kernel, capacity),
        out_shape=jax.ShapeDtypeStruct(
            (starts.shape[1], substeps, capacity // LANES, LANES), jnp.int32
        ),
        in_specs=[pl.BlockSpec(memory_space=pltpu.SMEM), vmem],
        out_specs=vmem,
        name="cut_requests",
    )(starts, ordered.reshape(substeps, rows, LANES))


def plan(feet, cross_dev, along_dev):
    along_count = lax.axis_size("along")
    across_count = lax.axis_size("across")
    cells = cross_dev * along_dev
    reach = along_count // 8
    capacity = 9 * cells // (8 * across_count * reach)
    span = 2 * reach - 1
    partners = across_count * span
    substeps = feet.shape[0]
    owner_along, owner_across, local_cell = owners(
        feet.reshape(substeps, cells), cross_dev, along_dev, along_dev * along_count
    )
    offset = owner_along - lax.axis_index("along")
    partner = owner_across * span + offset + reach - 1
    key = (partner * cells + jnp.arange(cells, dtype=jnp.int32)) * cells + local_cell
    ordered = [jnp.pad(lax.sort(key[s]) % cells, (0, capacity)) for s in range(substeps)]
    labels = jnp.arange(partners, dtype=jnp.int32)[:, None]
    member = (partner[:, None, :] == labels).astype(jnp.int32)
    rank, counts = prefix_count(member.reshape(substeps * partners, cells))
    rank = rank.reshape(substeps, partners, cells)
    target = jnp.sum(member * (rank + capacity * labels), axis=1)
    counts = counts.reshape(substeps, partners)
    starts = jnp.cumsum(counts, axis=1) - counts
    if capacity % LANES == 0:
        requests = cut_requests(jnp.stack(ordered), starts, capacity)
        return requests.reshape(across_count, span, substeps, capacity), target
    requests = [
        lax.dynamic_slice(ordered[s], (starts[s, p],), (capacity,))
        for p in range(partners)
        for s in range(substeps)
    ]
    return jnp.stack(requests).reshape(across_count, span, substeps, capacity), target


def hop_groups(reach, power):
    upward = [offset + reach - 1 for offset in range(1 - reach, 0) if -offset >> power & 1]
    downward = [offset + reach - 1 for offset in range(1, reach) if offset >> power & 1]
    return (upward, downward)


UNROLL = 32


def gather_kernel(index_ref, table_ref, out_ref):
    def step(i, carry):
        base = pl.multiple_of(i * UNROLL, UNROLL)
        for u in range(UNROLL):
            out_ref[pl.ds(base + u, 1), :] = table_ref[pl.ds(index_ref[base + u], 1), :]
        return carry

    lax.fori_loop(0, out_ref.shape[0] // UNROLL, step, 0)


def gather_rows(table, index):
    count, width = index.shape[0], table.shape[1]
    return pl.pallas_call(
        gather_kernel,
        out_shape=jax.ShapeDtypeStruct((count, width), table.dtype),
        in_specs=[
            pl.BlockSpec(memory_space=pltpu.SMEM),
            pl.BlockSpec(memory_space=pltpu.VMEM),
        ],
        out_specs=pl.BlockSpec(memory_space=pltpu.VMEM),
        name="gather_rows",
    )(index, table)


def blend_kernel(layers, index_ref, table_ref, fraction_ref, out_ref):
    width = out_ref.shape[1]
    lane = lax.broadcasted_iota(jnp.int32, (UNROLL, width), 1)
    top = lane % layers == layers - 1

    def step(i, carry):
        base = pl.multiple_of(i * UNROLL, UNROLL)
        for u in range(UNROLL):
            out_ref[pl.ds(base + u, 1), :] = table_ref[pl.ds(index_ref[base + u], 1), :]
        rows = out_ref[pl.ds(base, UNROLL), :]
        upper = jnp.where(top, rows, pltpu.roll(rows, width - 1, 1))
        weight = fraction_ref[pl.ds(base, UNROLL), :]
        out_ref[pl.ds(base, UNROLL), :] = (1.0 - weight) * rows + weight * upper
        return carry

    lax.fori_loop(0, out_ref.shape[0] // UNROLL, step, 0)


def blend_rows(table, index, fraction, layers):
    return pl.pallas_call(
        functools.partial(blend_kernel, layers),
        out_shape=jax.ShapeDtypeStruct(fraction.shape, table.dtype),
        in_specs=[
            pl.BlockSpec(memory_space=pltpu.SMEM),
            pl.BlockSpec(memory_space=pltpu.VMEM),
            pl.BlockSpec(memory_space=pltpu.VMEM),
        ],
        out_specs=pl.BlockSpec(memory_space=pltpu.VMEM),
        name="blend_rows",
    )(index, table, fraction)


def to_holders(requests):
    reach = (requests.shape[1] + 1) // 2
    moved = lax.all_to_all(requests, "across", split_axis=0, concat_axis=0, tiled=True)
    for power in range((reach - 1).bit_length()):
        upward, downward = hop_groups(reach, power)
        moved = moved.at[:, upward].set(shifted(moved[:, upward], "along", -(1 << power)))
        moved = moved.at[:, downward].set(shifted(moved[:, downward], "along", 1 << power))
    return moved


def to_askers(picked):
    reach = (picked.shape[1] + 1) // 2
    for power in range((reach - 1).bit_length()):
        upward, downward = hop_groups(reach, power)
        picked = picked.at[:, upward].set(shifted(picked[:, upward], "along", 1 << power))
        picked = picked.at[:, downward].set(shifted(picked[:, downward], "along", -(1 << power)))
    return lax.all_to_all(picked, "across", split_axis=0, concat_axis=0, tiled=True)


PIECES = 3
MESH = pl.DeviceIdType.MESH


def blend(rows, weight, top):
    upper = jnp.where(top, rows, pltpu.roll(rows, rows.shape[1] - 1, 1))
    return (1.0 - weight) * rows + weight * upper


def exchange_kernel(
    layers,
    components,
    cross_dev,
    capacity,
    target_ref,
    requests_ref,
    fields_hbm,
    first_hbm,
    second_hbm,
    out_ref,
    west_ref,
    east_ref,
    north_ref,
    south_ref,
    fields_ref,
    first_ref,
    second_ref,
    asked_vmem,
    asked,
    table,
    first_rows,
    second_rows,
    sent_1,
    sent_2,
    raw_1,
    raw_2,
    back_1,
    back_2,
    stage,
    stage_weight,
    final,
    ask_send,
    ask_recv,
    ask_local,
    send_sem,
    recv_sem,
    load_sem,
    edge_w,
    edge_e,
    halo_n,
    halo_s,
    halo_w,
    halo_e,
    halo_send,
    halo_recv,
):
    tiles = fields_ref.shape[0]
    along_dev = tiles * LANES
    cells = cross_dev * along_dev
    width = table.shape[1]
    blocks = capacity // LANES
    piece = capacity // PIECES
    along = lax.axis_index("along")
    me = lax.axis_index("across")
    peers = [lax.rem(me + 2, 4), 3 - me, me + 1 - 2 * lax.rem(me, 2)]
    pad = jnp.zeros((width - layers * components, LANES), jnp.float32)
    top = lax.broadcasted_iota(jnp.int32, (LANES, width), 1) % layers == layers - 1

    loads = [
        [
            pltpu.make_async_copy(
                source.at[:, pl.ds(t * LANES, LANES)], place.at[t], load_sem.at[s, t]
            )
            for t in range(tiles)
        ]
        for s, (source, place) in enumerate(
            [(fields_hbm, fields_ref), (first_hbm, first_ref), (second_hbm, second_ref)]
        )
    ]
    for group in loads:
        for copy in group:
            copy.start()

    barrier = pltpu.get_barrier_semaphore()
    for peer in peers:
        pl.semaphore_signal(barrier, inc=1, device_id=(along, peer), device_id_type=MESH)
    along_count = lax.axis_size("along")
    has_west, has_east = along > 0, along < along_count - 1
    has_north, has_south = me > 0, me < lax.axis_size("across") - 1

    @pl.when(has_west)
    def _():
        pl.semaphore_signal(barrier, inc=1, device_id=(along - 1, me), device_id_type=MESH)

    @pl.when(has_east)
    def _():
        pl.semaphore_signal(barrier, inc=1, device_id=(along + 1, me), device_id_type=MESH)

    pl.semaphore_wait(barrier, 3 + has_west.astype(jnp.int32) + has_east.astype(jnp.int32))

    asks = []
    for j, peer in enumerate(peers):
        copy = pltpu.make_async_remote_copy(
            src_ref=requests_ref.at[peer],
            dst_ref=asked_vmem.at[me],
            send_sem=ask_send.at[j],
            recv_sem=ask_recv.at[j],
            device_id=(along, peer),
            device_id_type=MESH,
        )
        copy.start()
        asks.append(copy)
    own = pltpu.make_async_copy(requests_ref.at[me], asked.at[me], ask_local.at[3])
    own.start()

    for copy in loads[0]:
        copy.wait()

    def fill_table(i, carry):
        for t in range(tiles):
            parts = [
                fields_ref[t, pl.ds(m * cross_dev + i, layers, stride=components * cross_dev), :]
                for m in range(components)
            ]
            rows = jnp.concatenate(parts + [pad], axis=0).T
            table[pl.ds(pl.multiple_of(i * along_dev + t * LANES, LANES), LANES), :] = rows
        return carry

    lax.fori_loop(0, cross_dev, fill_table, 0)

    def fill_weight(source, rows_ref):
        def step(i, carry):
            for t in range(tiles):
                part = source[t, pl.ds(i, layers, stride=cross_dev), :]
                rows = jnp.concatenate([part] * components + [pad], axis=0).T
                rows_ref[pl.ds(pl.multiple_of(i * along_dev + t * LANES, LANES), LANES), :] = rows
            return carry

        lax.fori_loop(0, cross_dev, step, 0)

    locals_ = []
    for j, peer in enumerate(peers):
        asks[j].wait_recv()
        copy = pltpu.make_async_copy(asked_vmem.at[peer], asked.at[peer], ask_local.at[j])
        copy.start()
        locals_.append(copy)
    for copy in locals_ + [own]:
        copy.wait()

    steps = piece // LANES

    def gather_1(peer, row):
        for u in range(LANES):
            stage[pl.ds(u, 1), :] = table[pl.ds(asked[peer, row, u], 1), :]
        return stage[...]

    def gather_2(peer, row):
        for u in range(LANES):
            cell = asked[peer, blocks + row, u]
            stage[pl.ds(u, 1), :] = back_1[pl.ds(target_ref[0, cell], 1), :]
            stage_weight[pl.ds(u, 1), :] = first_rows[pl.ds(cell, 1), :]
        return blend(stage[...], stage_weight[...], top)

    def exchange(gather, phase, sent, raw, back, beside):
        copies = [(j, c) for c in range(PIECES) for j in range(2)]
        copies += [(2, c) for c in range(PIECES)]
        started = []
        waiting = None
        for j, c in copies:
            slot = j * PIECES + c

            def step(b, carry, j=j, c=c, slot=slot):
                columns = gather(peers[j], c * steps + b).T[: layers * components]
                sent[slot, :, pl.ds(pl.multiple_of(b * LANES, LANES), LANES)] = columns
                return carry

            lax.fori_loop(0, steps, step, 0)
            copy = pltpu.make_async_remote_copy(
                src_ref=sent.at[slot],
                dst_ref=raw.at[slot],
                send_sem=send_sem.at[phase, j, c],
                recv_sem=recv_sem.at[phase, j, c],
                device_id=(along, peers[j]),
                device_id_type=MESH,
            )
            if waiting is not None:
                waiting.start()
            waiting = copy
            started.append(copy)

        def keep(b, carry):
            rows = pl.ds(pl.multiple_of(me * capacity + b * LANES, LANES), LANES)
            back[rows, :] = gather(me, b)
            return carry

        lax.fori_loop(0, 1, keep, 0)
        waiting.start()
        lax.fori_loop(1, blocks, keep, 0)
        beside()
        for (j, c), copy in zip(copies, started):
            copy.wait_recv()

            def restore(b, carry, j=j, c=c):
                lanes = pl.ds(pl.multiple_of(b * LANES, LANES), LANES)
                start = peers[j] * capacity + c * piece + b * LANES
                columns = raw[j * PIECES + c, :, lanes]
                rows = jnp.concatenate([columns, pad], axis=0).T
                back[pl.ds(pl.multiple_of(start, LANES), LANES), :] = rows
                return carry

            lax.fori_loop(0, steps, restore, 0)
        for copy in started:
            copy.wait_send()

    def weights():
        for copy in loads[1] + loads[2]:
            copy.wait()
        fill_weight(first_ref, first_rows)
        fill_weight(second_ref, second_rows)

    exchange(gather_1, 0, sent_1, raw_1, back_1, weights)
    exchange(gather_2, 1, sent_2, raw_2, back_2, lambda: None)

    def unpack(start):
        start = pl.multiple_of(start, LANES)
        for u in range(LANES):
            final[pl.ds(start + u, 1), :] = back_2[pl.ds(target_ref[1, start + u], 1), :]
        rows = pl.ds(start, LANES)
        final[rows, :] = blend(final[rows, :], second_rows[rows, :], top)

    def unpack_row(first):
        def step(t, carry):
            unpack(first + t * LANES)
            return carry

        lax.fori_loop(0, tiles, step, 0)

    def halo(j, source, place, peer):
        return pltpu.make_async_remote_copy(
            src_ref=source,
            dst_ref=place,
            send_sem=halo_send.at[j],
            recv_sem=halo_recv.at[j],
            device_id=peer,
            device_id_type=MESH,
        )

    top_row, last_row = pl.ds(0, along_dev), pl.ds(cells - along_dev, along_dev)
    north = halo(0, final.at[top_row], halo_s, (along, me - 1))
    south = halo(1, final.at[last_row], halo_n, (along, me + 1))
    west = halo(2, edge_w, halo_e, (along - 1, me))
    east = halo(3, edge_e, halo_w, (along + 1, me))

    unpack_row(0)
    unpack_row(cells - along_dev)
    inner = cross_dev - 2

    def outer_columns(i, carry):
        unpack((i + 1) * along_dev)
        unpack((i + 2) * along_dev - LANES)
        return carry

    lax.fori_loop(0, inner, outer_columns, 0)

    for i in range(cross_dev):
        edge_w[pl.ds(i, 1), :] = final[pl.ds(i * along_dev, 1), :]
        edge_e[pl.ds(i, 1), :] = final[pl.ds((i + 1) * along_dev - 1, 1), :]

    for present, copy in [
        (has_north, north), (has_south, south), (has_west, west), (has_east, east)
    ]:
        @pl.when(present)
        def _(copy=copy):
            copy.start()

    def inner_columns(i, carry):
        def step(t, carry):
            unpack((i + 1) * along_dev + (t + 1) * LANES)
            return carry

        return lax.fori_loop(0, tiles - 2, step, carry)

    lax.fori_loop(0, inner, inner_columns, 0)

    def spread(value, ref, first, stride, t):
        for m in range(components):
            ref[t, pl.ds(m * stride + first, layers, stride=components * stride), :] = value[
                m * layers : (m + 1) * layers
            ]

    def emit(i, carry):
        for t in range(tiles):
            rows = pl.ds(pl.multiple_of(i * along_dev + t * LANES, LANES), LANES)
            spread(final[rows, :].T, out_ref, i, cross_dev, t)
        return carry

    lax.fori_loop(0, cross_dev, emit, 0)

    for present, copy, place in [
        (has_south, north, halo_s),
        (has_north, south, halo_n),
        (has_east, west, halo_e),
        (has_west, east, halo_w),
    ]:
        @pl.when(present)
        def _(copy=copy):
            copy.wait_recv()

        @pl.when(jnp.logical_not(present))
        def _(place=place):
            place[...] = jnp.zeros_like(place)

    for t in range(tiles):
        rows = pl.ds(t * LANES, LANES)
        spread(halo_n[rows, :].T, north_ref, 0, 1, t)
        spread(halo_s[rows, :].T, south_ref, 0, 1, t)
    for i in range(cross_dev):
        for source, place in [(halo_w, west_ref), (halo_e, east_ref)]:
            row = jnp.broadcast_to(source[pl.ds(i, 1), :], (LANES, width))
            spread(row.T, place, i, cross_dev, 0)

    for present, copy in [
        (has_north, north), (has_south, south), (has_west, west), (has_east, east)
    ]:
        @pl.when(present)
        def _(copy=copy):
            copy.wait_send()

    for copy in asks:
        copy.wait_send()


def advect_twice(fields, requests, target, first_fraction, second_fraction):
    layers, components, cross_dev, along_dev = fields.shape
    cells = cross_dev * along_dev
    partners, substeps, capacity = requests.shape
    width = (layers * components + LANES - 1) // LANES * LANES
    vmem = pl.BlockSpec(memory_space=pltpu.VMEM)
    smem = pl.BlockSpec(memory_space=pltpu.SMEM)
    hbm = pl.BlockSpec(memory_space=pl.ANY)
    tiles = along_dev // LANES
    grid = requests.reshape(partners, substeps * capacity // LANES, LANES)
    rows = lambda count: pltpu.VMEM((count, width), jnp.float32)
    shape = lambda *dims: jax.ShapeDtypeStruct(dims, jnp.float32)
    edge = layers * components
    columns = pltpu.VMEM((3 * PIECES, edge, capacity // PIECES), jnp.float32)
    return pl.pallas_call(
        functools.partial(exchange_kernel, layers, components, cross_dev, capacity),
        out_shape=[
            shape(tiles, edge * cross_dev, LANES),
            shape(1, edge * cross_dev, LANES),
            shape(1, edge * cross_dev, LANES),
            shape(tiles, edge, LANES),
            shape(tiles, edge, LANES),
        ],
        in_specs=[smem, vmem, hbm, hbm, hbm],
        out_specs=[vmem] * 5,
        scratch_shapes=[
            pltpu.VMEM((tiles, layers * components * cross_dev, LANES), jnp.float32),
            pltpu.VMEM((tiles, layers * cross_dev, LANES), jnp.float32),
            pltpu.VMEM((tiles, layers * cross_dev, LANES), jnp.float32),
            pltpu.VMEM(grid.shape, jnp.int32),
            pltpu.SMEM(grid.shape, jnp.int32),
            rows(cells),
            rows(cells),
            rows(cells),
            columns,
            columns,
            columns,
            columns,
            rows(4 * capacity),
            rows(4 * capacity),
            rows(LANES),
            rows(LANES),
            rows(cells),
            pltpu.SemaphoreType.DMA((3,)),
            pltpu.SemaphoreType.DMA((3,)),
            pltpu.SemaphoreType.DMA((4,)),
            pltpu.SemaphoreType.DMA((2, 3, PIECES)),
            pltpu.SemaphoreType.DMA((2, 3, PIECES)),
            pltpu.SemaphoreType.DMA((3, tiles)),
            rows(cross_dev),
            rows(cross_dev),
            rows(along_dev),
            rows(along_dev),
            rows(cross_dev),
            rows(cross_dev),
            pltpu.SemaphoreType.DMA((4,)),
            pltpu.SemaphoreType.DMA((4,)),
        ],
        compiler_params=pltpu.CompilerParams(collective_id=0, has_side_effects=True),
        name="advect_twice",
    )(
        target,
        grid,
        fields.reshape(layers * components * cross_dev, along_dev),
        first_fraction.reshape(layers * cross_dev, along_dev),
        second_fraction.reshape(layers * cross_dev, along_dev),
    )


def solve_kernel(
    layers,
    components,
    moved_ref,
    west_ref,
    east_ref,
    north_ref,
    south_ref,
    present_ref,
    lateral_ref,
    mix_ref,
    drag_ref,
    stress_ref,
    out_ref,
    factors,
):
    cross_dev = out_ref.shape[2]
    tiles = moved_ref.shape[0]
    lane = lax.broadcasted_iota(jnp.int32, (cross_dev, LANES), 1)
    row = lax.broadcasted_iota(jnp.int32, (cross_dev, LANES), 0)
    at = [pl.ds(t * LANES, LANES) for t in range(tiles)]
    lateral = [lateral_ref[:, at[t]] for t in range(tiles)]
    present = [present_ref[:, at[t]] for t in range(tiles)]

    def mixed(k, m):
        level = k * components + m
        rows = pl.ds(pl.multiple_of(level * cross_dev, cross_dev), cross_dev)
        here = [moved_ref[t, rows, :] for t in range(tiles)]
        right = [pltpu.roll(x, 1, 1) for x in [west_ref[0, rows, :]] + here]
        left = [pltpu.roll(x, LANES - 1, 1) for x in here + [east_ref[0, rows, :]]]
        result = []
        for t in range(tiles):
            x = here[t]
            before = jnp.where(lane == 0, right[t], right[t + 1])
            after = jnp.where(lane == LANES - 1, left[t + 1], left[t])
            above = jnp.where(
                row == 0, north_ref[t, pl.ds(level, 1), :], pltpu.roll(x, 1, 0)
            )
            below = jnp.where(
                row == cross_dev - 1,
                south_ref[t, pl.ds(level, 1), :],
                pltpu.roll(x, cross_dev - 1, 0),
            )
            total = above + below + before + after
            result.append(x + lateral[t] * (total - present[t] * x))
        return result

    def forward(k, carry, first=False, final=False):
        factor, partial = carry or (None, None)
        source = [mixed(k, m) for m in range(components)]
        new_factor, new_partial = [], [None] * components
        for g in range(2):
            members = (0, 1) if g == 0 else (2,)
            row_factor = []
            for t in range(tiles):
                above = 0.0 if final else mix_ref[g, k, :, at[t]]
                below = 0.0 if first else mix_ref[g, k - 1, :, at[t]]
                diagonal = 1.0 + below + above
                if first:
                    if g == 0:
                        diagonal = diagonal + drag_ref[:, at[t]]
                else:
                    diagonal = diagonal - below * factor[g][t]
                inverse = 1.0 / diagonal
                for m in members:
                    value = source[m][t]
                    if final and g == 0:
                        value = value + stress_ref[m, :, at[t]]
                    if not first:
                        value = value + below * partial[m][t]
                    value = value * inverse
                    new_partial[m] = (new_partial[m] or []) + [value]
                    out_ref[k, m, :, at[t]] = value
                if not final:
                    ratio = above * inverse
                    factors[g, k, :, at[t]] = ratio
                    row_factor.append(ratio)
            new_factor.append(row_factor)
        return new_factor, new_partial

    carry = forward(0, None, first=True)
    carry = lax.fori_loop(1, layers - 1, forward, carry)
    _, value = forward(layers - 1, carry, final=True)

    def backward(step, value):
        k = layers - 2 - step
        result = []
        for m in range(components):
            g = 0 if m < 2 else 1
            level = []
            for t in range(tiles):
                x = out_ref[k, m, :, at[t]] + factors[g, k, :, at[t]] * value[m][t]
                out_ref[k, m, :, at[t]] = x
                level.append(x)
            result.append(level)
        return result

    lax.fori_loop(0, layers - 1, backward, value)


def mix_and_solve(pieces, present, lateral_mix, vertical_mix, bottom_drag, surface_stress, shape):
    layers, components, cross_dev, along_dev = shape
    vmem = pl.BlockSpec(memory_space=pltpu.VMEM)
    return pl.pallas_call(
        functools.partial(solve_kernel, layers, components),
        out_shape=jax.ShapeDtypeStruct(shape, jnp.float32),
        in_specs=[vmem] * 10,
        out_specs=vmem,
        scratch_shapes=[pltpu.VMEM((2, layers - 1, cross_dev, along_dev), jnp.float32)],
        name="mix_and_solve",
    )(*pieces, present, lateral_mix, vertical_mix, bottom_drag, surface_stress)


def body(
    fields,
    first_feet,
    first_fraction,
    second_feet,
    second_fraction,
    lateral_mix,
    vertical_mix,
    bottom_drag,
    surface_stress,
):
    layers, components, cross_dev, along_dev = fields.shape
    cells = cross_dev * along_dev
    row_count = layers * components
    width = (row_count + 127) // 128 * 128

    requests, target = plan(jnp.stack([first_feet, second_feet]), cross_dev, along_dev)
    across_count, span, substeps, capacity = requests.shape

    row_total = cross_dev * lax.axis_size("across")
    column_total = along_dev * lax.axis_size("along")
    row_index = lax.axis_index("across") * cross_dev + jnp.arange(cross_dev, dtype=jnp.int32)
    column_index = lax.axis_index("along") * along_dev + jnp.arange(along_dev, dtype=jnp.int32)
    row_present = (row_index > 0).astype(jnp.float32) + (row_index < row_total - 1).astype(
        jnp.float32
    )
    column_present = (column_index > 0).astype(jnp.float32) + (
        column_index < column_total - 1
    ).astype(jnp.float32)
    present = row_present[:, None] + column_present[None, :]
    if span == 1 and across_count == 4 and capacity % (PIECES * LANES) == 0:
        pieces = advect_twice(fields, requests[:, 0], target, first_fraction, second_fraction)
        return mix_and_solve(
            pieces,
            present,
            lateral_mix,
            vertical_mix,
            bottom_drag,
            surface_stress,
            fields.shape,
        )
    else:
        asked = to_holders(requests.reshape(across_count, span, substeps * capacity))

        def advect(table, asked, target, fraction):
            weight = jnp.pad(
                jnp.tile(fraction.reshape(layers, cells), (components, 1)),
                ((0, width - row_count), (0, 0)),
            ).T
            picked = gather_rows(table, asked.reshape(-1))
            returned = to_askers(picked.reshape(asked.shape + (width,)))
            return blend_rows(returned.reshape(-1, width), target, weight, layers)

        table = fields.transpose(1, 0, 2, 3).reshape(row_count, cells)
        table = jnp.pad(table, ((0, width - row_count), (0, 0))).T
        middle = advect(table, asked[:, :, :capacity], target[0], first_fraction)
        moved = advect(middle, asked[:, :, capacity:], target[1], second_fraction)
        moved = moved.T[:row_count].reshape(components, layers, cross_dev, along_dev)
        moved = moved.transpose(1, 0, 2, 3)
    padded = padded_2(moved, (("across", 2), ("along", 3)), 1)
    beside_all = neighbour_sum(padded)
    mixed = moved + lateral_mix * (beside_all - present * moved)
    return solve_columns(mixed, vertical_mix, bottom_drag, surface_stress)


def solution(mesh):
    in_specs = (
        P(None, None, "across", "along"),
        P("across", "along"),
        P(None, "across", "along"),
        P("across", "along"),
        P(None, "across", "along"),
        P("across", "along"),
        P(None, None, "across", "along"),
        P("across", "along"),
        P(None, "across", "along"),
    )
    out_specs = P(None, None, "across", "along")
    return jax.shard_map(body, mesh=mesh, in_specs=in_specs, out_specs=out_specs, check_vma=False)
```
